32 devices in a mesh: dp: 4 (over y, x), seq: 8 (over z, core).
Axes of the slice: x: 2, y: 2, z: 4, core: 2. Of those that a mesh axis runs over, the one named last changes fastest.
Arguments:
- features: bfloat16 [32, 16, 32, 512], P('dp', 'seq'), may hold values from -6 to 6
- conv_weight: bfloat16 [3, 3, 3, 16, 512], replicated, may hold values from -0.0546875 to 0.0546875
- clip_frames: int32 [8], replicated, may hold values from 1 to 7, as said below
- clip_group: int32 [8], replicated, may hold values from 0 to 3, as said below
- clip_offset: int32 [8], replicated, may hold values from 0 to 7, as said below
- clip_times: float32 [8], replicated, may hold values from 0.05 to 0.95
- noise_tokens: bfloat16 [4, 1024, 64], P('dp', 'seq'), may hold values from -6 to 6
- embed_weight: bfloat16 [64, 2048], replicated, may hold values from -0.75 to 0.75
- attention_proj: bfloat16 [2048, 3, 8, 128], P(None, None, 'seq'), may hold values from -0.125 to 0.125
- norm_gains: float32 [2, 128], replicated, may hold values from 0.5 to 1.5
- cotangent: bfloat16 [4, 1024, 1024], P('dp', 'seq'), may hold values from -0.09375 to 0.09375
Outputs:
- noisy_tokens: float32 [4, 1024, 64], P('dp', 'seq')
- attention_out: bfloat16 [4, 1024, 1024], P('dp', 'seq')
- proj_grad: float32 [2048, 3, 8, 128], P('dp', None, 'seq')
- norm_grad: float32 [2, 128], replicated
The draws below stay inside these ranges and needn't reach their ends.
Inputs may be any that keep to these rules, and one draw needn't show every extreme that they name: `clip_frames`: clips follow one another along time from frame 0 and together cover all 32 frames. `clip_group`: every group trains on exactly two clips, whose frames add up to 8. `clip_offset`: the clips of one group take consecutive frame slots from slot 0 in their time order and fill all 8 slots of the group.
All inputs are finite; a program needn't handle non-finite values.
Results may differ from the reference program's by a relative error of at most 0.014.
Values may be sent and summed in bfloat16 or wider, within the bound.
No kernel may reach another device: no remote copies, remote signals or barrier semaphores. Data moves between devices by JAX's collectives and lax.ppermute only.
A program may use at most 128 MiB of HBM per device.

```python
import jax
import jax.numpy as jnp
from jax import lax

D = 2048
HEAD_DIM = 128
CIN = 512
LAT = 16
WD = 32
FR_DEV = 8
HEADS = 8
HT = 16
TPR = 16
TOK_DEV = 128
SEQLEN = 1024
FRAMES = 32
CLIPS = 8
N_DP = 4
N_SEQ = 8


def clip_plan(key):
    base_key = jax.random.fold_in(key, 11)
    key_order, key_sizes = jax.random.split(base_key, 2)
    group_count = CLIPS // 2
    order = jax.random.permutation(key_order, group_count).astype(jnp.int32)
    owners = jnp.concatenate([order, order]).astype(jnp.int32)
    first_len = jax.random.randint(key_sizes, (group_count,), 1, FR_DEV).astype(jnp.int32)
    positions = jnp.arange(group_count).astype(jnp.int32)
    first_len = jnp.where(positions == 0, FR_DEV - 1, jnp.where(positions == group_count - 1, 1, first_len)).astype(jnp.int32)
    lengths = jnp.concatenate([first_len, FR_DEV - first_len]).astype(jnp.int32)
    offsets = jnp.concatenate([jnp.zeros((group_count,), jnp.int32), first_len]).astype(jnp.int32)
    return (lengths, owners, offsets)


def draw_clip_frames(key, part):
    return clip_plan(key)[0]


def draw_clip_group(key, part):
    return clip_plan(key)[1]


def draw_clip_offset(key, part):
    return clip_plan(key)[2]


def block_scale(rng, dims, cuts, low, largest):
    def one(axis_at, parts):
        heights = jax.random.uniform(jax.random.fold_in(jax.random.fold_in(rng, 6), axis_at), (parts,), jnp.float32, low / len(cuts), largest / len(cuts))
        return jnp.repeat(jnp.exp(heights), dims[axis_at] // parts).reshape((-1,) + (1,) * (len(dims) - axis_at - 1))

    level = one(*cuts[0])
    for cut in cuts[1:]:
        level = level * one(*cut)
    return level


def centred(own_key, extent, width, limit, pieces=(), kind=jnp.bfloat16):
    drawn = width * jax.random.normal(own_key, extent, jnp.float32)
    if pieces:
        drawn = drawn * block_scale(own_key, extent, pieces, -0.22, 0.18)
    return jnp.clip(drawn, -limit, limit).astype(kind)


def setup_inputs(seed: int = 0) -> dict:
    splits = jax.random.split(jax.random.key(seed), 12)
    features = centred(splits[0], (FRAMES, HT, WD, CIN), 1.0, 6.0, ((0, 4), (1, 8)))
    conv_weight = centred(splits[1], (3, 3, 3, LAT, CIN), (27 * CIN) ** -0.5, 0.0546875)
    clip_frames = draw_clip_frames(jax.random.fold_in(splits[11], 71), 0)
    clip_group = draw_clip_group(jax.random.fold_in(splits[11], 71), 0)
    clip_offset = draw_clip_offset(jax.random.fold_in(splits[11], 71), 0)
    clip_times = jnp.clip(jax.random.uniform(splits[5], (CLIPS,), jnp.float32, 0.05, 0.95), 0.05, 0.95)
    noise_tokens = centred(splits[6], (N_DP, SEQLEN, 4 * LAT), 1.0, 6.0, ((0, 4), (1, 8)))
    embed_weight = centred(splits[7], (4 * LAT, D), (4 * LAT) ** -0.5, 0.75)
    attention_proj = centred(splits[8], (D, 3, HEADS, HEAD_DIM), D ** -0.5, 0.125, ((2, 8),))
    norm_gains = jnp.clip(1.0 + 0.1 * jax.random.normal(splits[9], (2, HEAD_DIM), jnp.float32), 0.5, 1.5)
    cotangent = centred(splits[10], (N_DP, SEQLEN, HEADS * HEAD_DIM), (1.0 / (N_DP * SEQLEN) ** 0.5), 0.09375, ((0, 4), (1, 8)))
    return {"features": features, "conv_weight": conv_weight, "clip_frames": clip_frames, "clip_group": clip_group, "clip_offset": clip_offset, "clip_times": clip_times, "noise_tokens": noise_tokens, "embed_weight": embed_weight, "attention_proj": attention_proj, "norm_gains": norm_gains, "cotangent": cotangent}


def clip_bounds(clip_frames):
    ends_at = jnp.cumsum(clip_frames).astype(jnp.int32)
    return ((ends_at - clip_frames).astype(jnp.int32), ends_at)

def frame_start(frame_ids, starts_at, ends_at):
    member = (frame_ids[:, None] >= starts_at[None, :]) & (frame_ids[:, None] < ends_at[None, :])
    own_start = lax.optimization_barrier(jnp.sum(jnp.where(member, starts_at[None, :], 0), axis=1)).astype(jnp.int32)
    return (own_start, member)

def slot_table(group_id, slot_ids, clip_group, clip_offset, clip_frames, starts_at, clip_times):
    member = (clip_group[None, :] == group_id) & (slot_ids[:, None] >= clip_offset[None, :]) & (slot_ids[:, None] < clip_offset[None, :] + clip_frames[None, :])
    numbers = jnp.arange(clip_frames.shape[0]).astype(jnp.int32)
    usable = jnp.any(member, axis=1).astype(jnp.float32)
    segment = (lax.optimization_barrier(jnp.sum(jnp.where(member, numbers[None, :] + 1, 0), axis=1)) - 1).astype(jnp.int32)
    source = lax.optimization_barrier(jnp.sum(jnp.where(member, starts_at[None, :] + slot_ids[:, None] - clip_offset[None, :], 0), axis=1)).astype(jnp.int32)
    noise_level = lax.optimization_barrier(jnp.sum(jnp.where(member, clip_times[None, :], jnp.zeros((), clip_times.dtype)), axis=1))
    return (usable, segment, source, noise_level)

def rms_scale(values, gain_row):
    inverse = lax.rsqrt(lax.optimization_barrier(jnp.mean(values * values, axis=-1, keepdims=True)) + 1e-06)
    return (values * inverse * gain_row, inverse)

def rms_back(values, inverse, gain_row, upstream):
    scaled = gain_row * upstream
    grad_in = inverse * scaled - values * inverse ** 3 * lax.optimization_barrier(jnp.mean(values * scaled, axis=-1, keepdims=True))
    gain_part = lax.optimization_barrier(jnp.sum(upstream * values * inverse, axis=(0, 1)))
    return (grad_in, gain_part)

def head_pass(operands):
    queries, key_rows, value_rows, grad_rows, segment_ids = operands
    score_scale = HEAD_DIM ** (-0.5)
    same_clip = segment_ids[:, None] == segment_ids[None, :]
    scores = jnp.dot(queries, key_rows.T, preferred_element_type=jnp.float32) * score_scale
    exp_scores = jnp.where(same_clip, jnp.exp(scores), 0.0)
    prob_rows = exp_scores / lax.optimization_barrier(jnp.sum(exp_scores, axis=1, keepdims=True))
    probs_bf = prob_rows.astype(jnp.bfloat16)
    output = jnp.dot(probs_bf, value_rows, preferred_element_type=jnp.float32)
    prob_grad = jnp.dot(grad_rows, value_rows.T, preferred_element_type=jnp.float32)
    row_delta = lax.optimization_barrier(jnp.sum(prob_rows * prob_grad, axis=1, keepdims=True))
    score_grad = (prob_rows * (prob_grad - row_delta) * score_scale).astype(jnp.bfloat16)
    query_grad = jnp.dot(score_grad, key_rows, preferred_element_type=jnp.float32)
    key_grad = jnp.dot(score_grad.T, queries, preferred_element_type=jnp.float32)
    value_grad = jnp.dot(probs_bf.T, grad_rows, preferred_element_type=jnp.float32)
    return (output, query_grad, key_grad, value_grad)

def reference(features, conv_weight, clip_frames, clip_group, clip_offset, clip_times, noise_tokens, embed_weight, attention_proj, norm_gains, cotangent):
    starts_at, ends_at = clip_bounds(clip_frames)
    frame_ids = jnp.arange(FRAMES).astype(jnp.int32)
    own_start, member = frame_start(frame_ids, starts_at, ends_at)
    activated = jax.nn.silu(features.astype(jnp.float32)).astype(jnp.bfloat16)
    padded = jnp.pad(activated, ((2, 0), (1, 1), (1, 1), (0, 0)))
    latent = jnp.zeros((FRAMES * HT * WD, LAT), jnp.float32)
    for tap_time in range(3):
        allowed = (frame_ids - (2 - tap_time) >= own_start).astype(jnp.float32)
        allowed_rows = jnp.repeat(allowed, HT * WD)[:, None]
        for tap_row in range(3):
            for tap_col in range(3):
                tap_piece = padded[tap_time:tap_time + FRAMES, tap_row:tap_row + HT, tap_col:tap_col + WD].reshape(-1, CIN)
                tap_term = jnp.dot(tap_piece, conv_weight[tap_time, tap_row, tap_col].T, preferred_element_type=jnp.float32)
                latent = latent + allowed_rows * tap_term
    patches = latent.reshape(FRAMES, N_SEQ, 2, TPR, 2, LAT).transpose(0, 1, 3, 2, 4, 5).reshape(FRAMES, N_SEQ, TPR, 4 * LAT)
    slot_ids = jnp.arange(FR_DEV).astype(jnp.int32)
    group_ids = jnp.arange(N_DP).astype(jnp.int32)
    usable, segment, source, noise_level = jax.vmap(slot_table, in_axes=(0, None, None, None, None, None, None))(group_ids, slot_ids, clip_group, clip_offset, clip_frames, starts_at, clip_times)
    picked = patches[source].transpose(0, 2, 1, 3, 4).reshape(N_DP, SEQLEN, 4 * LAT)
    slot_of_token = (jnp.arange(SEQLEN) % TOK_DEV // TPR).astype(jnp.int32)
    tok_usable = usable[:, slot_of_token]
    tok_level = noise_level[:, slot_of_token]
    tok_segment = segment[:, slot_of_token]
    noisy_tokens = tok_usable[..., None] * ((1.0 - tok_level[..., None]) * picked + tok_level[..., None] * noise_tokens.astype(jnp.float32))
    proj_flat = attention_proj.reshape(D, 3 * HEADS * HEAD_DIM)

    def group_step(running, inputs):
        proj_acc, gain_acc = running
        tokens_group, usable_group, segment_group, cot_group = inputs
        hidden = jnp.dot(tokens_group.astype(jnp.bfloat16), embed_weight, preferred_element_type=jnp.float32).astype(jnp.bfloat16)
        mixed_all = jnp.dot(hidden, proj_flat, preferred_element_type=jnp.float32).reshape(SEQLEN, 3, HEADS, HEAD_DIM)
        query_n, query_inv = rms_scale(mixed_all[:, 0], norm_gains[0])
        key_n, key_inv = rms_scale(mixed_all[:, 1], norm_gains[1])
        query_bf = query_n.astype(jnp.bfloat16)
        key_bf = key_n.astype(jnp.bfloat16)
        value_bf = mixed_all[:, 2].astype(jnp.bfloat16)
        incoming = jnp.where(usable_group[:, None, None] > 0, cot_group.reshape(SEQLEN, HEADS, HEAD_DIM), jnp.zeros((), jnp.bfloat16))
        segments_h = jnp.broadcast_to(segment_group[None, :], (HEADS, SEQLEN))
        output, query_grad, key_grad, value_grad = lax.map(head_pass, (query_bf.transpose(1, 0, 2), key_bf.transpose(1, 0, 2), value_bf.transpose(1, 0, 2), incoming.transpose(1, 0, 2), segments_h))
        attention_group = (usable_group[:, None, None] * output.transpose(1, 0, 2)).astype(jnp.bfloat16).reshape(SEQLEN, HEADS * HEAD_DIM)
        query_in, query_gain = rms_back(mixed_all[:, 0], query_inv, norm_gains[0], query_grad.transpose(1, 0, 2))
        key_in, key_gain = rms_back(mixed_all[:, 1], key_inv, norm_gains[1], key_grad.transpose(1, 0, 2))
        stacked = jnp.stack([query_in, key_in, value_grad.transpose(1, 0, 2)], axis=1).astype(jnp.bfloat16).reshape(SEQLEN, 3 * HEADS * HEAD_DIM)
        proj_term = lax.dot_general(hidden, stacked, (((0,), (0,)), ((), ())), preferred_element_type=jnp.float32)
        return ((proj_acc + proj_term, gain_acc + jnp.stack([query_gain, key_gain])), attention_group)
    start_state = (jnp.zeros((D, 3 * HEADS * HEAD_DIM), jnp.float32), jnp.zeros((2, HEAD_DIM), jnp.float32))
    final_state, attention_out = lax.scan(group_step, start_state, (noisy_tokens, tok_usable, tok_segment, cotangent))
    proj_grad = final_state[0].reshape(D, 3, HEADS, HEAD_DIM)
    return (noisy_tokens, attention_out, proj_grad, final_state[1])
```

```python
import functools

import jax
import jax.numpy as jnp
from jax import lax
from jax.experimental import pallas as pl
from jax.experimental.pallas import tpu as pltpu
from jax.sharding import PartitionSpec as P


F32 = jnp.float32
BF16 = jnp.bfloat16
LOG2E = 1.4426950408889634
EPS = 1e-06
BIG = 16384.0
CELLS = ((0, 0), (0, 1), (1, 0), (1, 1), (2, 0), (2, 1), (-1, 0), (-1, 1))
NT = (((1,), (1,)), ((), ()))
TN = (((0,), (0,)), ((), ()))


def swap(block, axis, mask):
    return lax.ppermute(block, axis, [(i, i ^ mask) for i in range(lax.axis_size(axis))])


def cost(flops, moved, exps=0):
    return pl.CostEstimate(flops=int(flops), bytes_accessed=int(moved), transcendentals=int(exps))


def params(mib=48):
    return pltpu.CompilerParams(vmem_limit_bytes=mib * 1024 * 1024)


VMEM = pl.BlockSpec(memory_space=pltpu.VMEM)
SMEM = pl.BlockSpec(memory_space=pltpu.SMEM)


def split(x):
    high = x.astype(BF16)
    return high, (x - high.astype(F32)).astype(BF16)


def conv_kernel(dims, frames_ref, feat_ref, w_ref, cot_ref, part_ref, *rest):
    fr, wd, ch, lat, clips, n_seq, head = dims
    cot_refs, (act_ref, wst_ref) = rest[:n_seq], rest[n_seq:]
    cols = wd // 2
    slab = lax.axis_index("dp")
    me = lax.axis_index("seq")
    for m in range(n_seq):
        at = pl.multiple_of((me ^ m) * head, head)
        cot_refs[m][...] = cot_ref[:, pl.ds(at, head)]
    lanes = len(CELLS) * lat
    for row in range(2):
        for par in range(2):
            for dt in range(3):
                for blk in range(2):
                    for g, (out_row, out_par) in enumerate(CELLS):
                        dr = row - out_row
                        valid = abs(dr) <= 1
                        dw = par - out_par
                        if blk == 1:
                            valid = valid and dw != 0
                            dw = -dw
                        at = (dt * 2 + blk) * lanes + g * lat
                        tap = ((2 - dt) * 3 + dr + 1) * 3 + dw + 1
                        wst_ref[row * 2 + par, at : at + lat, :] = (
                            w_ref[tap * lat : (tap + 1) * lat, :]
                            if valid
                            else jnp.zeros((lat, ch), BF16)
                        )
    raw = feat_ref[...].astype(F32)
    act = raw / (1.0 + jnp.exp(-raw))
    for i in range(ch // 128):
        act_ref[i] = act[:, i * 128 : (i + 1) * 128]
    half = fr * 2 * cols
    total = None
    for par in range(2):
        mine = jnp.concatenate(
            [
                act_ref[i, pl.ds(par, half, stride=2), :].astype(BF16)
                for i in range(ch // 128)
            ],
            axis=1,
        ).reshape(fr, 2, cols, ch)
        for row in range(2):
            term = lax.dot_general(
                mine[:, row].reshape(fr * cols, ch),
                wst_ref[row * 2 + par],
                NT,
                preferred_element_type=F32,
            )
            total = term if total is None else total + term
    starts = [jnp.int32(0)] * (fr + 2)
    begin = jnp.int32(0)
    for c in range(clips):
        end = begin + frames_ref[c]
        for f in range(fr + 2):
            t = slab * fr + f
            starts[f] = jnp.where((t >= begin) & (t < end), begin, starts[f])
        begin = end
    sums = []
    for blk in range(2):
        pieces = []
        for f in range(fr + 2):
            piece = jnp.zeros((cols, lanes), F32)
            for dt in range(3):
                src = f - dt
                if 0 <= src < fr:
                    keep = (slab * fr + src >= starts[f]).astype(F32)
                    at = (dt * 2 + blk) * lanes
                    piece = piece + keep * total[src * cols : (src + 1) * cols, at : at + lanes]
            pieces.append(piece)
        sums.append(jnp.concatenate(pieces, axis=0))
    same, side = sums
    rows = (fr + 2) * cols
    col_at = lax.broadcasted_iota(jnp.int32, (rows, lanes), 0) % cols
    par_at = (lax.broadcasted_iota(jnp.int32, (rows, lanes), 1) // lat) % 2
    after = jnp.where(col_at < cols - 1, pltpu.roll(side, rows - 1, 0), 0.0)
    before = jnp.where(col_at > 0, pltpu.roll(side, 1, 0), 0.0)
    part_ref[...] = (same + jnp.where(par_at == 1, after, before)).astype(BF16)


def slot_scan(fr, clips, slab, frames_ref, group_ref, offset_ref, times_ref=None):
    source = [jnp.int32(-1)] * fr
    owner = [jnp.int32(clips)] * fr
    level = [jnp.float32(0.0)] * fr
    usable = [jnp.float32(0.0)] * fr
    begin = jnp.int32(0)
    for c in range(clips):
        size, off = frames_ref[c], offset_ref[c]
        here = group_ref[c] == slab
        for f in range(fr):
            member = here & (off <= f) & (f < off + size)
            source[f] = jnp.where(member, begin + f - off, source[f])
            owner[f] = jnp.where(member, c, owner[f])
            usable[f] = jnp.where(member, 1.0, usable[f])
            if times_ref is not None:
                level[f] = jnp.where(member, times_ref[c], level[f])
        begin = begin + size
    return source, owner, usable, level


def slot_kernel(dims, frames_ref, group_ref, offset_ref, times_ref, noise_ref, *rest):
    fr, cols, clips, n_dp, patch = dims
    part_refs, (send_ref, own_ref) = rest[:n_dp], rest[n_dp:]
    slab = lax.axis_index("dp")
    source, _, usable, level = slot_scan(
        fr, clips, slab, frames_ref, group_ref, offset_ref, times_ref
    )
    noise = noise_ref[...].astype(F32).T
    lanes = part_refs[0].shape[1]
    noise = jnp.concatenate([noise, jnp.zeros((noise.shape[0], lanes - patch), F32)], axis=1)
    for f in range(fr):
        got = jnp.zeros((cols, lanes), F32)
        for m in range(n_dp):
            at = source[f] - (slab ^ m) * fr
            valid = ((at >= 0) & (at < fr + 2) & (source[f] >= 0)).astype(F32)
            at = pl.multiple_of(jnp.clip(at, 0, fr + 1) * cols, cols)
            got = got + valid * part_refs[m][pl.ds(at, cols), :].astype(F32)
        here = slice(f * cols, (f + 1) * cols)
        own = usable[f] * ((1.0 - level[f]) * got + level[f] * noise[here])
        own_ref[here, :] = own
        send_ref[here, :] = own.astype(BF16)


def weight_kernel(embed_ref, proj_ref, out_ref):
    head = proj_ref.shape[2]
    patch = embed_ref.shape[0]
    for i in range(3):
        both = jnp.dot(embed_ref[...], proj_ref[i], preferred_element_type=F32)
        high, low = split(both)
        out_ref[:patch, i * head : (i + 1) * head] = high
        out_ref[patch:, i * head : (i + 1) * head] = low


def attention_kernel(dims, frames_ref, group_ref, offset_ref, gains_ref, w_ref, own_ref, *rest):
    fr, cols, clips, n_seq, patch, head, tile = dims
    tok_refs, cot_refs = rest[:n_seq], rest[n_seq : 2 * n_seq]
    rest = rest[2 * n_seq :]
    noisy_ref, grad_ref, gain_ref = rest[:3]
    out_refs = rest[3 : 3 + n_seq]
    rest = rest[3 + n_seq :]
    tok_ref, inc_ref, x_ref, q_ref, k_ref, v_ref, o_ref, dq_ref, dk_ref, dv_ref = rest
    slab = lax.axis_index("dp")
    me = lax.axis_index("seq")
    blk = fr * cols
    size = n_seq * blk
    width = 2 * patch
    _, owner, usable, _ = slot_scan(fr, clips, slab, frames_ref, group_ref, offset_ref)
    live = jnp.concatenate([jnp.full((cols, head), u, F32) for u in usable], axis=0)
    lane = lax.broadcasted_iota(jnp.int32, (cols, head), 1)
    mark = jnp.concatenate([(lane == o).astype(F32) for o in owner], axis=0)
    tok_ref[:blk, :] = jnp.zeros((blk, width), BF16)
    tok_ref[size + blk :, :] = jnp.zeros((blk, width), BF16)
    for m in range(n_seq):
        at = pl.multiple_of((me ^ m) * blk, blk)
        tok_ref[pl.ds(at + blk, blk), :] = tok_refs[m][...]
        inc_ref[pl.ds(at, blk), :] = (cot_refs[m][...].astype(F32) * live).astype(BF16)
    own_at = pl.multiple_of(me * blk, blk)
    lane_b = lax.broadcasted_iota(jnp.int32, (blk, width), 1)
    side = jnp.where(
        lane_b < patch + patch // 2,
        tok_ref[pl.ds(own_at, blk), :].astype(F32),
        tok_ref[pl.ds(own_at + 2 * blk, blk), :].astype(F32),
    )
    noisy = own_ref[...] + pltpu.roll(side, patch, 1)
    noisy_ref[...] = noisy.T[:patch, :]

    ones = jnp.full((2 * head, head), 1.0 / head, BF16)

    def mean(values):
        return jnp.dot(
            jnp.concatenate(split(values), axis=1), ones, preferred_element_type=F32
        )

    weights = w_ref[...]
    toks = []
    for p in range(n_seq):
        rows = slice(p * blk, (p + 1) * blk)
        side = jnp.where(
            lane_b < patch + patch // 2,
            tok_ref[rows, :].astype(F32),
            tok_ref[(p + 2) * blk : (p + 3) * blk, :].astype(F32),
        )
        tok = tok_ref[(p + 1) * blk : (p + 2) * blk, :].astype(F32) + pltpu.roll(side, patch, 1)
        tok = jnp.where(lane_b < patch, tok, pltpu.roll(tok, patch, 1)).astype(BF16)
        toks.append(tok)
        x_ref[rows, :] = jnp.dot(tok, weights, preferred_element_type=F32)
    for p in range(n_seq):
        rows = slice(p * blk, (p + 1) * blk)
        x = x_ref[rows, :head]
        scale = lax.rsqrt(mean(x * x) + EPS)
        q_ref[rows, :head] = (x * scale * (gains_ref[0:1, :] * (head**-0.5 * LOG2E))).astype(BF16)
        q_ref[rows, head:] = mark.astype(BF16)
        x = x_ref[rows, head : 2 * head]
        scale = lax.rsqrt(mean(x * x) + EPS)
        k_ref[rows, :head] = (x * scale * gains_ref[1:2, :]).astype(BF16)
        k_ref[rows, head:] = ((mark - 1.0) * BIG).astype(BF16)
        v_ref[rows, :head] = x_ref[rows, 2 * head :].astype(BF16)
        v_ref[rows, head:] = jnp.ones((blk, head), BF16)
    dk_ref[...] = jnp.zeros_like(dk_ref)
    dv_ref[...] = jnp.zeros_like(dv_ref)

    def step(i, carry):
        rows = pl.ds(pl.multiple_of(i * tile, tile), tile)
        scores = lax.dot_general(q_ref[rows, :], k_ref[...], NT, preferred_element_type=F32)
        exps = jnp.exp2(scores)
        exps_bf = exps.astype(BF16)
        both = jnp.dot(exps_bf, v_ref[...], preferred_element_type=F32)
        inverse = 1.0 / both[:, head:]
        output = both[:, :head] * inverse
        o_ref[rows, :] = output.astype(BF16)
        scaled = inc_ref[rows, :].astype(F32) * inverse
        scaled_bf = scaled.astype(BF16)
        upstream = jnp.concatenate([scaled_bf, (-(scaled * output)).astype(BF16)], axis=1)
        prob_grad = lax.dot_general(upstream, v_ref[...], NT, preferred_element_type=F32)
        score_grad = (exps * prob_grad).astype(BF16)
        dq_ref[rows, :] = jnp.dot(score_grad, k_ref[:, :head], preferred_element_type=F32)
        dk_ref[...] += lax.dot_general(
            score_grad, q_ref[rows, :head], TN, preferred_element_type=F32
        )
        dv_ref[...] += lax.dot_general(exps_bf, scaled_bf, TN, preferred_element_type=F32)
        return carry

    lax.fori_loop(0, size // tile, step, 0)

    gains = []
    grad = None
    for p in range(n_seq):
        rows = slice(p * blk, (p + 1) * blk)
        parts = []
        for i, (ref, unit) in enumerate(((dq_ref, head**-0.5), (dk_ref, 1.0 / LOG2E))):
            x = x_ref[rows, i * head : (i + 1) * head]
            up = ref[rows, :] * unit
            scale = lax.rsqrt(mean(x * x) + EPS)
            unit_x = x * scale
            gain_up = up * gains_ref[i : i + 1, :]
            parts.append((scale * (gain_up - unit_x * mean(unit_x * gain_up))).astype(BF16))
            add = jnp.sum(up * unit_x, axis=0, keepdims=True)
            if p == 0:
                gains.append(add)
            else:
                gains[i] = gains[i] + add
        parts.append(dv_ref[rows, :].astype(BF16))
        term = lax.dot_general(
            toks[p], jnp.concatenate(parts, axis=1), TN, preferred_element_type=F32
        )
        grad = term if grad is None else grad + term
    grad_ref[...] = grad[:patch, :].astype(BF16)
    gain_ref[...] = jnp.concatenate(gains, axis=0)
    for m in range(n_seq):
        at = pl.multiple_of((me ^ m) * blk, blk)
        out_refs[m][...] = (o_ref[pl.ds(at, blk), :].astype(F32) * live).astype(BF16)


def proj_kernel(dims, embed_ref, *rest):
    n_dp, patch, head, rows = dims
    grad_refs, (out_ref,) = rest[:n_dp], rest[n_dp:]
    slab = lax.axis_index("dp")
    part = embed_ref[:, pl.ds(pl.multiple_of(slab * rows, rows), rows)]
    left = jnp.concatenate([part] * n_dp, axis=0)
    right = jnp.concatenate([ref[...] for ref in grad_refs], axis=0)
    result = lax.dot_general(left, right, TN, preferred_element_type=F32)
    for i in range(3):
        out_ref[pl.ds(i, rows, stride=3), :] = result[:, i * head : (i + 1) * head]


def finish_kernel(dims, sums_ref, *rest):
    n_seq, head, devices = dims
    out_refs, (out_ref, gain_ref) = rest[:n_seq], rest[n_seq:]
    me = lax.axis_index("seq")
    for m in range(n_seq):
        at = pl.multiple_of((me ^ m) * head, head)
        out_ref[:, pl.ds(at, head)] = out_refs[m][...]
    gain_ref[...] = jnp.sum(sums_ref[...], axis=0)


def body(
    features,
    conv_weight,
    clip_frames,
    clip_group,
    clip_offset,
    clip_times,
    noise_tokens,
    embed_weight,
    attention_proj,
    norm_gains,
    cotangent,
):
    n_dp, n_seq = lax.axis_size("dp"), lax.axis_size("seq")
    fr, rows_dev, wd, ch = features.shape
    lat = conv_weight.shape[3]
    clips = clip_frames.shape[0]
    cols = wd // 2
    blk, patch = noise_tokens.shape[1:]
    model, _, heads_dev, head = attention_proj.shape
    assert rows_dev == 2 and heads_dev == 1 and blk == fr * cols and patch == 4 * lat
    size = n_seq * blk
    lanes = len(CELLS) * lat
    S = jax.ShapeDtypeStruct

    first = pl.pallas_call(
        functools.partial(conv_kernel, (fr, wd, ch, lat, clips, n_seq, head)),
        out_shape=[S(((fr + 2) * cols, lanes), BF16)] + [S((blk, head), BF16)] * n_seq,
        in_specs=[SMEM, VMEM, VMEM, VMEM],
        out_specs=[VMEM] * (1 + n_seq),
        scratch_shapes=[
            pltpu.VMEM((ch // 128, fr * 2 * wd, 128), F32),
            pltpu.VMEM((4, 6 * lanes, ch), BF16),
        ],
        compiler_params=params(),
        cost_estimate=cost(2 * fr * cols * 4 * ch * 6 * lanes, 2**21, fr * 2 * wd * ch),
        name="conv",
    )(
        clip_frames,
        features.reshape(fr * 2 * wd, ch),
        conv_weight.reshape(27 * lat, ch),
        cotangent.reshape(blk, n_seq * head),
    )
    partial, cot_out = first[0], first[1:]
    parts = [partial] + [swap(partial, "dp", m) for m in range(1, n_dp)]
    cots = [cot_out[0]] + [swap(cot_out[m], "seq", m) for m in range(1, n_seq)]

    weights = pl.pallas_call(
        weight_kernel,
        out_shape=S((2 * patch, 3 * head), BF16),
        in_specs=[VMEM] * 2,
        out_specs=VMEM,
        compiler_params=params(),
        cost_estimate=cost(2 * patch * model * 3 * head, 2 * model * (3 * head + patch)),
        name="weights",
    )(embed_weight, attention_proj.transpose(1, 2, 0, 3).reshape(3, model, head))

    send, own = pl.pallas_call(
        functools.partial(slot_kernel, (fr, cols, clips, n_dp, patch)),
        out_shape=[S((blk, lanes), BF16), S((blk, lanes), F32)],
        in_specs=[SMEM] * 4 + [VMEM] * (1 + n_dp),
        out_specs=[VMEM] * 2,
        compiler_params=params(),
        cost_estimate=cost(2**20, 2**18),
        name="slots",
    )(clip_frames, clip_group, clip_offset, clip_times, noise_tokens[0].T, *parts)
    toks = [send] + [None] * (n_seq - 1)
    for m in range(2, n_seq, 2):
        toks[m] = swap(send, "seq", m)
    for m in range(0, n_seq, 2):
        toks[m + 1] = swap(toks[m], "seq", 1)

    tile = min(256, size)
    third = pl.pallas_call(
        functools.partial(attention_kernel, (fr, cols, clips, n_seq, patch, head, tile)),
        out_shape=[S((patch, blk), F32), S((patch, 3 * head), BF16), S((2, head), F32)]
        + [S((blk, head), BF16)] * n_seq,
        in_specs=[SMEM] * 3 + [VMEM] * (3 + 2 * n_seq),
        out_specs=[VMEM] * (3 + n_seq),
        scratch_shapes=[
            pltpu.VMEM((size + 2 * blk, lanes), BF16),
            pltpu.VMEM((size, head), BF16),
            pltpu.VMEM((size, 3 * head), F32),
            pltpu.VMEM((size, 2 * head), BF16),
            pltpu.VMEM((size, 2 * head), BF16),
            pltpu.VMEM((size, 2 * head), BF16),
            pltpu.VMEM((size, head), BF16),
            pltpu.VMEM((size, head), F32),
            pltpu.VMEM((size, head), F32),
            pltpu.VMEM((size, head), F32),
        ],
        compiler_params=params(),
        cost_estimate=cost(12 * size * size * head, 2**21, size * size),
        name="attention",
    )(clip_frames, clip_group, clip_offset, norm_gains, weights, own, *toks, *cots)
    noisy, grad, gain, outs = third[0], third[1], third[2], third[3:]

    grads = [grad] + [swap(grad, "dp", m) for m in range(1, n_dp)]
    heads = [outs[0]] + [swap(outs[m], "seq", m) for m in range(1, n_seq)]
    devices = n_dp * n_seq
    gain_all = lax.all_to_all(
        jnp.broadcast_to(gain[None], (devices, 2, head)),
        ("dp", "seq"),
        split_axis=0,
        concat_axis=0,
        tiled=True,
    )
    rows = model // n_dp
    proj_grad = pl.pallas_call(
        functools.partial(proj_kernel, (n_dp, patch, head, rows)),
        out_shape=S((rows * 3, head), F32),
        in_specs=[VMEM] * (1 + n_dp),
        out_specs=VMEM,
        compiler_params=params(),
        cost_estimate=cost(2 * rows * 3 * head * patch * n_dp, 4 * rows * 3 * head),
        name="projgrad",
    )(embed_weight, *grads)
    out, norm_grad = pl.pallas_call(
        functools.partial(finish_kernel, (n_seq, head, devices)),
        out_shape=[S((blk, n_seq * head), BF16), S((2, head), F32)],
        in_specs=[VMEM] * (1 + n_seq),
        out_specs=[VMEM] * 2,
        compiler_params=params(),
        cost_estimate=cost(0, 4 * blk * n_seq * head),
        name="finish",
    )(gain_all, *heads)
    return (
        noisy.T[None],
        out[None],
        proj_grad.reshape(rows, 3, heads_dev, head),
        norm_grad,
    )


def solution(mesh):
    return jax.shard_map(
        body,
        mesh=mesh,
        in_specs=(
            P("dp", "seq", None, None),
            P(),
            P(),
            P(),
            P(),
            P(),
            P("dp", "seq", None),
            P(),
            P(None, None, "seq", None),
            P(),
            P("dp", "seq", None),
        ),
        out_specs=(P("dp", "seq", None), P("dp", "seq", None), P("dp", None, "seq", None), P()),
        check_vma=False,
    )
```

```python
import functools

import jax
import jax.numpy as jnp
from jax import lax
from jax.experimental import pallas as pl
from jax.experimental.pallas import tpu as pltpu
from jax.sharding import PartitionSpec as P


F32 = jnp.float32
BF16 = jnp.bfloat16
LOG2E = 1.4426950408889634
EPS = 1e-06
BIG = 16384.0
CELLS = ((0, 0), (0, 1), (1, 0), (1, 1), (2, 0), (2, 1), (-1, 0), (-1, 1))
NT = (((1,), (1,)), ((), ()))
TN = (((0,), (0,)), ((), ()))


def swap(block, axis, mask):
    return lax.ppermute(block, axis, [(i, i ^ mask) for i in range(lax.axis_size(axis))])


def keep_in(space, *arrays):
    return [pltpu.with_memory_space_constraint(a, space) for a in arrays]


def cost(flops, moved, exps=0):
    return pl.CostEstimate(flops=int(flops), bytes_accessed=int(moved), transcendentals=int(exps))


def params(mib=48):
    return pltpu.CompilerParams(vmem_limit_bytes=mib * 1024 * 1024)


VMEM = pl.BlockSpec(memory_space=pltpu.VMEM)
HBM = pl.BlockSpec(memory_space=pltpu.HBM)


def split(x):
    high = x.astype(BF16)
    return high, (x - high.astype(F32)).astype(BF16)


def split_kernel(dims, cot_hbm, cots_ref, sems):
    n_seq, head = dims
    loads = [
        pltpu.make_async_copy(
            cot_hbm.at[:, h * head : (h + 1) * head], cots_ref.at[h], sems.at[h]
        )
        for h in range(n_seq)
    ]
    for load in loads:
        load.start()
    for load in loads:
        load.wait()


def conv_kernel(dims, frames_hbm, feat_hbm, w_hbm, part_ref, *rest):
    fr, wd, ch, lat, clips = dims
    frames_ref, feat_ref, w_ref, act_ref, wst_ref, sems = rest
    cols = wd // 2
    slab = lax.axis_index("dp")
    loads = [
        pltpu.make_async_copy(w_hbm, w_ref, sems.at[0]),
        pltpu.make_async_copy(feat_hbm, feat_ref, sems.at[1]),
        pltpu.make_async_copy(frames_hbm, frames_ref, sems.at[2]),
    ]
    for load in loads:
        load.start()
    loads[0].wait()
    lanes = len(CELLS) * lat
    for row in range(2):
        for par in range(2):
            for dt in range(3):
                for blk in range(2):
                    for g, (out_row, out_par) in enumerate(CELLS):
                        dr = row - out_row
                        valid = abs(dr) <= 1
                        dw = par - out_par
                        if blk == 1:
                            valid = valid and dw != 0
                            dw = -dw
                        at = (dt * 2 + blk) * lanes + g * lat
                        tap = ((2 - dt) * 3 + dr + 1) * 3 + dw + 1
                        wst_ref[row * 2 + par, at : at + lat, :] = (
                            w_ref[tap * lat : (tap + 1) * lat, :]
                            if valid
                            else jnp.zeros((lat, ch), BF16)
                        )
    loads[1].wait()
    raw = feat_ref[...].astype(F32)
    act = raw / (1.0 + jnp.exp(-raw))
    for i in range(ch // 128):
        act_ref[i] = act[:, i * 128 : (i + 1) * 128]
    half = fr * 2 * cols
    total = None
    for par in range(2):
        mine = jnp.concatenate(
            [
                act_ref[i, pl.ds(par, half, stride=2), :].astype(BF16)
                for i in range(ch // 128)
            ],
            axis=1,
        ).reshape(fr, 2, cols, ch)
        for row in range(2):
            term = lax.dot_general(
                mine[:, row].reshape(fr * cols, ch),
                wst_ref[row * 2 + par],
                NT,
                preferred_element_type=F32,
            )
            total = term if total is None else total + term
    loads[2].wait()
    starts = [jnp.int32(0)] * (fr + 2)
    begin = jnp.int32(0)
    for c in range(clips):
        end = begin + frames_ref[c]
        for f in range(fr + 2):
            t = slab * fr + f
            starts[f] = jnp.where((t >= begin) & (t < end), begin, starts[f])
        begin = end
    sums = []
    for blk in range(2):
        pieces = []
        for f in range(fr + 2):
            piece = jnp.zeros((cols, lanes), F32)
            for dt in range(3):
                src = f - dt
                if 0 <= src < fr:
                    keep = (slab * fr + src >= starts[f]).astype(F32)
                    at = (dt * 2 + blk) * lanes
                    piece = piece + keep * total[src * cols : (src + 1) * cols, at : at + lanes]
            pieces.append(piece)
        sums.append(jnp.concatenate(pieces, axis=0))
    same, side = sums
    rows = (fr + 2) * cols
    col_at = lax.broadcasted_iota(jnp.int32, (rows, lanes), 0) % cols
    par_at = (lax.broadcasted_iota(jnp.int32, (rows, lanes), 1) // lat) % 2
    after = jnp.where(col_at < cols - 1, pltpu.roll(side, rows - 1, 0), 0.0)
    before = jnp.where(col_at > 0, pltpu.roll(side, 1, 0), 0.0)
    part_ref[...] = (same + jnp.where(par_at == 1, after, before)).astype(BF16)


def table_kernel(dims, after_ref, frames_hbm, group_hbm, offset_hbm, times_hbm, noise_hbm, *rest):
    fr, cols, clips, n_dp, patch, width = dims
    pick_ref, scale_ref, noise_ref, live_ref, mark_ref = rest[:5]
    frames_ref, group_ref, offset_ref, times_ref, raw_ref, sems = rest[5:]
    loads = [
        pltpu.make_async_copy(source, target, sems.at[i])
        for i, (source, target) in enumerate(
            (
                (frames_hbm, frames_ref),
                (group_hbm, group_ref),
                (offset_hbm, offset_ref),
                (times_hbm, times_ref),
                (noise_hbm, raw_ref),
            )
        )
    ]
    for load in loads:
        load.start()
    for load in loads:
        load.wait()
    slab = lax.axis_index("dp")
    source = [jnp.int32(-1)] * fr
    owner = [jnp.int32(clips)] * fr
    level = [jnp.float32(0.0)] * fr
    usable = [jnp.float32(0.0)] * fr
    begin = jnp.int32(0)
    for c in range(clips):
        size, off = frames_ref[c], offset_ref[c]
        here = group_ref[c] == slab
        for f in range(fr):
            member = here & (off <= f) & (f < off + size)
            source[f] = jnp.where(member, begin + f - off, source[f])
            owner[f] = jnp.where(member, c, owner[f])
            usable[f] = jnp.where(member, 1.0, usable[f])
            level[f] = jnp.where(member, times_ref[c], level[f])
        begin = begin + size
    rows = (fr + 2) * cols
    noise = raw_ref[...].astype(F32).T
    noise = jnp.concatenate([noise, jnp.zeros((fr * cols, width - patch), F32)], axis=1)
    ahead = lax.broadcasted_iota(jnp.int32, (cols, n_dp * rows), 1) - lax.broadcasted_iota(
        jnp.int32, (cols, n_dp * rows), 0
    )
    lane = lax.broadcasted_iota(jnp.int32, (cols, width), 1)
    for f in range(fr):
        here = slice(f * cols, (f + 1) * cols)
        hit = None
        for m in range(n_dp):
            at = source[f] - (slab ^ m) * fr
            valid = (at >= 0) & (at < fr + 2) & (source[f] >= 0)
            at = jnp.where(valid, m * rows + at * cols, -cols)
            hit = (ahead == at) if hit is None else hit | (ahead == at)
        pick_ref[here, :] = hit.astype(F32).astype(BF16)
        scale_ref[here, :] = jnp.full((cols, width), usable[f] * (1.0 - level[f]), F32)
        noise_ref[here, :] = (usable[f] * level[f]) * noise[here]
        live_ref[here, :] = jnp.full((cols, width), usable[f], F32)
        mark_ref[here, :] = (lane == owner[f]).astype(F32)


def slot_kernel(dims, pick_ref, scale_ref, noise_ref, *rest):
    (n_dp,) = dims
    part_refs, (send_ref, own_ref) = rest[:n_dp], rest[n_dp:]
    parts = jnp.concatenate([ref[...] for ref in part_refs], axis=0)
    got = jnp.dot(pick_ref[...], parts, preferred_element_type=F32)
    own = scale_ref[...] * got + noise_ref[...]
    own_ref[...] = own
    send_ref[...] = own.astype(BF16)


def weight_kernel(dims, after_ref, embed_hbm, proj_hbm, gains_hbm, out_ref, gains_ref, *rest):
    patch, head = dims
    embed_ref, proj_ref, sems = rest
    loads = [
        pltpu.make_async_copy(embed_hbm, embed_ref, sems.at[0]),
        pltpu.make_async_copy(gains_hbm, gains_ref, sems.at[1]),
    ] + [pltpu.make_async_copy(proj_hbm.at[i], proj_ref.at[i], sems.at[2 + i]) for i in range(3)]
    for load in loads:
        load.start()
    loads[0].wait()
    for i in range(3):
        loads[2 + i].wait()
        both = jnp.dot(embed_ref[...], proj_ref[i], preferred_element_type=F32)
        high, low = split(both)
        out_ref[:patch, i * head : (i + 1) * head] = high
        out_ref[patch:, i * head : (i + 1) * head] = low
    loads[1].wait()


def mean_of(values, head):
    ones = jnp.full((2 * head, head), 1.0 / head, BF16)
    return jnp.dot(jnp.concatenate(split(values), axis=1), ones, preferred_element_type=F32)


def attention_kernel(dims, gains_ref, w_ref, own_ref, live_ref, mark_ref, cots_ref, *rest):
    fr, cols, n_seq, patch, head, tile, devices = dims
    tok_refs, rest = rest[:n_seq], rest[n_seq:]
    noisy_ref, grad_ref, gain_ref = rest[:3]
    pairs_refs, rest = rest[3 : 3 + n_seq // 2], rest[3 + n_seq // 2 :]
    tok_ref, toks_ref, x_ref, q_ref, k_ref, v_ref, o_ref, dq_ref, dk_ref, dv_ref = rest
    me = lax.axis_index("seq")
    blk = fr * cols
    size = n_seq * blk
    width = 2 * patch
    tok_ref[:blk, :] = jnp.zeros((blk, width), BF16)
    tok_ref[size + blk :, :] = jnp.zeros((blk, width), BF16)
    for m in range(n_seq):
        at = pl.multiple_of((me ^ m) * blk, blk)
        tok_ref[pl.ds(at + blk, blk), :] = tok_refs[m][...]
    own_at = pl.multiple_of(me * blk, blk)
    lane = lax.broadcasted_iota(jnp.int32, (blk, width), 1)
    side = jnp.where(
        lane < patch + patch // 2,
        tok_ref[pl.ds(own_at, blk), :].astype(F32),
        tok_ref[pl.ds(own_at + 2 * blk, blk), :].astype(F32),
    )
    noisy = own_ref[...] + pltpu.roll(side, patch, 1)
    noisy_ref[...] = noisy.T[:patch, :]
    weights = w_ref[...]
    mark = mark_ref[...]
    for p in range(n_seq):
        rows = slice(p * blk, (p + 1) * blk)
        side = jnp.where(
            lane < patch + patch // 2,
            tok_ref[rows, :].astype(F32),
            tok_ref[(p + 2) * blk : (p + 3) * blk, :].astype(F32),
        )
        tok = tok_ref[(p + 1) * blk : (p + 2) * blk, :].astype(F32) + pltpu.roll(side, patch, 1)
        tok = jnp.where(lane < patch, tok, pltpu.roll(tok, patch, 1)).astype(BF16)
        toks_ref[rows, :] = tok
        x = jnp.dot(tok, weights, preferred_element_type=F32)
        x_ref[rows, :] = x
        scale = lax.rsqrt(mean_of(x[:, :head] * x[:, :head], head) + EPS)
        gain = gains_ref[0:1, :] * (head**-0.5 * LOG2E)
        q_ref[rows, :head] = (x[:, :head] * scale * gain).astype(BF16)
        q_ref[rows, head:] = mark.astype(BF16)
        x = x[:, head:]
        scale = lax.rsqrt(mean_of(x[:, :head] * x[:, :head], head) + EPS)
        k_ref[rows, :head] = (x[:, :head] * scale * gains_ref[1:2, :]).astype(BF16)
        k_ref[rows, head:] = ((mark - 1.0) * BIG).astype(BF16)
        v_ref[rows, :head] = x[:, head:].astype(BF16)
        v_ref[rows, head:] = jnp.ones((blk, head), BF16)
    per = tile // blk
    live = jnp.concatenate([live_ref[...]] * per, axis=0)
    for i in range(size // tile):
        rows = slice(i * tile, (i + 1) * tile)
        scores = lax.dot_general(q_ref[rows, :], k_ref[...], NT, preferred_element_type=F32)
        exps = jnp.exp2(scores)
        exps_bf = exps.astype(BF16)
        both = jnp.dot(exps_bf, v_ref[...], preferred_element_type=F32)
        inverse = 1.0 / both[:, head:]
        output = both[:, :head] * inverse
        o_ref[rows, :] = (output * live).astype(BF16)
        incoming = cots_ref[i * per : (i + 1) * per].reshape(tile, head)
        scaled = incoming.astype(F32) * live * inverse
        scaled_bf = scaled.astype(BF16)
        upstream = jnp.concatenate([scaled_bf, (-(scaled * output)).astype(BF16)], axis=1)
        prob_grad = lax.dot_general(upstream, v_ref[...], NT, preferred_element_type=F32)
        score_grad = (exps * prob_grad).astype(BF16)
        dq_ref[rows, :] = jnp.dot(score_grad, k_ref[:, :head], preferred_element_type=F32)
        dk = lax.dot_general(score_grad, q_ref[rows, :head], TN, preferred_element_type=F32)
        dv = lax.dot_general(exps_bf, scaled_bf, TN, preferred_element_type=F32)
        if i == 0:
            dk_ref[...] = dk
            dv_ref[...] = dv
        else:
            dk_ref[...] += dk
            dv_ref[...] += dv

    gains = []
    grad = None
    for p in range(n_seq):
        rows = slice(p * blk, (p + 1) * blk)
        parts = []
        for i, (ref, unit) in enumerate(((dq_ref, head**-0.5), (dk_ref, 1.0 / LOG2E))):
            x = x_ref[rows, i * head : (i + 1) * head]
            up = ref[rows, :] * unit
            scale = lax.rsqrt(mean_of(x * x, head) + EPS)
            unit_x = x * scale
            gain_up = up * gains_ref[i : i + 1, :]
            parts.append((scale * (gain_up - unit_x * mean_of(unit_x * gain_up, head))).astype(BF16))
            add = jnp.sum(up * unit_x, axis=0, keepdims=True)
            if p == 0:
                gains.append(add)
            else:
                gains[i] = gains[i] + add
        parts.append(dv_ref[rows, :].astype(BF16))
        term = lax.dot_general(
            toks_ref[rows, :], jnp.concatenate(parts, axis=1), TN, preferred_element_type=F32
        )
        grad = term if grad is None else grad + term
    grad_ref[...] = grad[:patch, :].astype(BF16)
    gain_ref[...] = jnp.broadcast_to(jnp.concatenate(gains, axis=0)[None], (devices, 2, head))
    for m in range(n_seq):
        at = pl.multiple_of((me ^ m) * blk, blk)
        pairs_refs[m // 2][m % 2] = o_ref[pl.ds(at, blk), :]


def proj_kernel(dims, embed_ref, *rest):
    n_dp, _, head, rows = dims
    grad_refs, (out_ref,) = rest[:n_dp], rest[n_dp:]
    slab = lax.axis_index("dp")
    part = embed_ref[:, pl.ds(pl.multiple_of(slab * rows, rows), rows)]
    left = jnp.concatenate([part] * n_dp, axis=0)
    right = jnp.concatenate([ref[...] for ref in grad_refs], axis=0)
    result = lax.dot_general(left, right, TN, preferred_element_type=F32)
    for i in range(3):
        out_ref[pl.ds(i, rows, stride=3), :] = result[:, i * head : (i + 1) * head]


def finish_kernel(dims, sums_ref, *rest):
    n_seq, head = dims
    own_refs, other_refs, (out_ref, gain_ref) = rest[: n_seq // 2], rest[n_seq // 2 : n_seq], rest[n_seq:]
    me = lax.axis_index("seq")
    for m in range(n_seq):
        at = pl.multiple_of((me ^ m) * head, head)
        source = other_refs if m % 2 else own_refs
        out_ref[:, pl.ds(at, head)] = source[m // 2][m % 2]
    gain_ref[...] = jnp.sum(sums_ref[...], axis=0)


def body(
    features,
    conv_weight,
    clip_frames,
    clip_group,
    clip_offset,
    clip_times,
    noise_tokens,
    embed_weight,
    attention_proj,
    norm_gains,
    cotangent,
):
    n_dp, n_seq = lax.axis_size("dp"), lax.axis_size("seq")
    fr, rows_dev, wd, ch = features.shape
    lat = conv_weight.shape[3]
    clips = clip_frames.shape[0]
    cols = wd // 2
    blk, patch = noise_tokens.shape[1:]
    model, _, heads_dev, head = attention_proj.shape
    assert rows_dev == 2 and heads_dev == 1 and blk == fr * cols and patch == 4 * lat
    size = n_seq * blk
    lanes = len(CELLS) * lat
    S = jax.ShapeDtypeStruct

    rows_out = (fr + 2) * cols
    tile = min(256, size)
    devices = n_dp * n_seq
    gather = dict(split_axis=0, concat_axis=0, tiled=True)

    cots = pl.pallas_call(
        functools.partial(split_kernel, (n_seq, head)),
        out_shape=S((n_seq, blk, head), BF16),
        in_specs=[HBM],
        out_specs=VMEM,
        scratch_shapes=[pltpu.SemaphoreType.DMA((n_seq,))],
        compiler_params=params(),
        cost_estimate=cost(0, 4 * blk * n_seq * head),
        name="split",
    )(*keep_in(pltpu.HBM, cotangent.reshape(blk, n_seq * head)))
    cots = lax.all_to_all(cots, "seq", **gather)

    partial = pl.pallas_call(
        functools.partial(conv_kernel, (fr, wd, ch, lat, clips)),
        out_shape=S((rows_out, lanes), BF16),
        in_specs=[HBM] * 3,
        out_specs=VMEM,
        scratch_shapes=[
            pltpu.SMEM((clips,), jnp.int32),
            pltpu.VMEM((fr * 2 * wd, ch), BF16),
            pltpu.VMEM((27 * lat, ch), BF16),
            pltpu.VMEM((ch // 128, fr * 2 * wd, 128), F32),
            pltpu.VMEM((4, 6 * lanes, ch), BF16),
            pltpu.SemaphoreType.DMA((3,)),
        ],
        compiler_params=params(),
        cost_estimate=cost(2 * fr * cols * 4 * ch * 6 * lanes, 2**21, fr * 2 * wd * ch),
        name="conv",
    )(
        *keep_in(
            pltpu.HBM,
            clip_frames,
            features.reshape(fr * 2 * wd, ch),
            conv_weight.reshape(27 * lat, ch),
        )
    )
    parts = [partial] + [swap(partial, "dp", m) for m in range(1, n_dp)]
    pick, scale, noise, live, mark = pl.pallas_call(
        functools.partial(table_kernel, (fr, cols, clips, n_dp, patch, lanes)),
        out_shape=[S((blk, n_dp * rows_out), BF16)] + [S((blk, lanes), F32)] * 4,
        in_specs=[VMEM] + [HBM] * 5,
        out_specs=[VMEM] * 5,
        scratch_shapes=[pltpu.SMEM((clips,), jnp.int32)] * 3
        + [
            pltpu.SMEM((clips,), F32),
            pltpu.VMEM((patch, blk), BF16),
            pltpu.SemaphoreType.DMA((5,)),
        ],
        compiler_params=params(),
        cost_estimate=cost(2**22, 2**21),
        name="tables",
    )(partial, clip_frames, clip_group, clip_offset, clip_times, noise_tokens[0].T)

    send, own = pl.pallas_call(
        functools.partial(slot_kernel, (n_dp,)),
        out_shape=[S((blk, lanes), BF16), S((blk, lanes), F32)],
        in_specs=[VMEM] * (3 + n_dp),
        out_specs=[VMEM] * 2,
        compiler_params=params(),
        cost_estimate=cost(2**20, 2**18),
        name="slots",
    )(pick, scale, noise, *parts)
    toks = [send] + [None] * (n_seq - 1)
    for m in range(2, n_seq, 2):
        toks[m] = swap(send, "seq", m)
    for m in range(0, n_seq, 2):
        toks[m + 1] = swap(toks[m], "seq", 1)
    weights, gains = pl.pallas_call(
        functools.partial(weight_kernel, (patch, head)),
        out_shape=[S((2 * patch, 3 * head), BF16), S((2, head), F32)],
        in_specs=[VMEM] + [HBM] * 3,
        out_specs=[VMEM] * 2,
        scratch_shapes=[
            pltpu.VMEM((patch, model), BF16),
            pltpu.VMEM((3, model, head), BF16),
            pltpu.SemaphoreType.DMA((5,)),
        ],
        compiler_params=params(),
        cost_estimate=cost(2 * patch * model * 3 * head, 2 * model * (3 * head + patch)),
        name="weights",
    )(send, embed_weight, attention_proj.transpose(1, 2, 0, 3).reshape(3, model, head), norm_gains)

    wide = 2 * head
    noisy, grad, gain, *pairs = pl.pallas_call(
        functools.partial(attention_kernel, (fr, cols, n_seq, patch, head, tile, devices)),
        out_shape=[S((patch, blk), F32), S((patch, 3 * head), BF16), S((devices, 2, head), F32)]
        + [S((2, blk, head), BF16)] * (n_seq // 2),
        in_specs=[VMEM] * (6 + n_seq),
        out_specs=[VMEM] * (3 + n_seq // 2),
        scratch_shapes=[
            pltpu.VMEM((size + 2 * blk, lanes), BF16),
            pltpu.VMEM((size, lanes), BF16),
            pltpu.VMEM((size, 3 * head), F32),
            pltpu.VMEM((size, wide), BF16),
            pltpu.VMEM((size, wide), BF16),
            pltpu.VMEM((size, wide), BF16),
            pltpu.VMEM((size, head), BF16),
            pltpu.VMEM((size, head), F32),
            pltpu.VMEM((size, head), F32),
            pltpu.VMEM((size, head), F32),
        ],
        compiler_params=params(),
        cost_estimate=cost(12 * size * size * head, 2**21, size * size),
        name="attention",
    )(gains, weights, own, live, mark, cots, *toks)

    grads = [grad] + [swap(grad, "dp", m) for m in range(1, n_dp)]
    gain_all = lax.all_to_all(gain, ("dp", "seq"), **gather)
    pairs = [pairs[0]] + [swap(pairs[m], "seq", 2 * m) for m in range(1, n_seq // 2)]
    others = [swap(pair, "seq", 1) for pair in pairs]
    rows = model // n_dp
    proj_grad = pl.pallas_call(
        functools.partial(proj_kernel, (n_dp, patch, head, rows)),
        out_shape=S((rows * 3, head), F32),
        in_specs=[VMEM] * (1 + n_dp),
        out_specs=VMEM,
        compiler_params=params(),
        cost_estimate=cost(2 * rows * 3 * head * patch * n_dp, 4 * rows * 3 * head),
        name="projgrad",
    )(embed_weight, *grads)
    out, norm_grad = pl.pallas_call(
        functools.partial(finish_kernel, (n_seq, head)),
        out_shape=[S((blk, n_seq * head), BF16), S((2, head), F32)],
        in_specs=[VMEM] * (1 + n_seq),
        out_specs=[VMEM] * 2,
        compiler_params=params(),
        cost_estimate=cost(0, 4 * blk * n_seq * head),
        name="finish",
    )(gain_all, *pairs, *others)
    return (
        noisy.T[None],
        out[None],
        proj_grad.reshape(rows, 3, heads_dev, head),
        norm_grad,
    )


def solution(mesh):
    return jax.shard_map(
        body,
        mesh=mesh,
        in_specs=(
            P("dp", "seq", None, None),
            P(),
            P(),
            P(),
            P(),
            P(),
            P("dp", "seq", None),
            P(),
            P(None, None, "seq", None),
            P(),
            P("dp", "seq", None),
        ),
        out_specs=(P("dp", "seq", None), P("dp", "seq", None), P("dp", None, "seq", None), P()),
        check_vma=False,
    )
```

```python
import functools

import jax
import jax.numpy as jnp
from jax import lax
from jax.experimental import pallas as pl
from jax.experimental.pallas import tpu as pltpu
from jax.sharding import PartitionSpec as P


F32 = jnp.float32
BF16 = jnp.bfloat16
LOG2E = 1.4426950408889634
EPS = 1e-06
BIG = 16384.0
EXTRA = 16
CELLS = ((0, 0), (0, 1), (1, 0), (1, 1), (2, 0), (2, 1), (-1, 0), (-1, 1))
NT = (((1,), (1,)), ((), ()))
TN = (((0,), (0,)), ((), ()))


def swap(block, axis, mask):
    return lax.ppermute(block, axis, [(i, i ^ mask) for i in range(lax.axis_size(axis))])


def keep_in(space, *arrays):
    return [pltpu.with_memory_space_constraint(a, space) for a in arrays]


def cost(flops, moved, exps=0):
    return pl.CostEstimate(flops=int(flops), bytes_accessed=int(moved), transcendentals=int(exps))


def params(mib=48):
    return pltpu.CompilerParams(vmem_limit_bytes=mib * 1024 * 1024)


VMEM = pl.BlockSpec(memory_space=pltpu.VMEM)
HBM = pl.BlockSpec(memory_space=pltpu.HBM)


def split_kernel(dims, cot_hbm, *rest):
    n_seq, head = dims
    pair_refs, sems = rest[: n_seq // 2], rest[n_seq // 2]
    me = lax.axis_index("seq")
    loads = []
    for m in range(n_seq):
        at = pl.multiple_of((me ^ m) * head, head)
        loads.append(
            pltpu.make_async_copy(
                cot_hbm.at[:, pl.ds(at, head)], pair_refs[m // 2].at[m % 2], sems.at[m]
            )
        )
    for load in loads:
        load.start()
    for load in loads:
        load.wait()


def conv_kernel(dims, frames_hbm, feat_hbm, w_hbm, part_ref, *rest):
    fr, wd, ch, lat, clips = dims
    frames_ref, feat_ref, w_ref, act_ref, wst_ref, sems = rest
    cols = wd // 2
    slab = lax.axis_index("dp")
    loads = [
        pltpu.make_async_copy(w_hbm, w_ref, sems.at[0]),
        pltpu.make_async_copy(feat_hbm, feat_ref, sems.at[1]),
        pltpu.make_async_copy(frames_hbm, frames_ref, sems.at[2]),
    ]
    for load in loads:
        load.start()
    loads[0].wait()
    lanes = len(CELLS) * lat
    for row in range(2):
        for par in range(2):
            for dt in range(3):
                for blk in range(2):
                    for g, (out_row, out_par) in enumerate(CELLS):
                        dr = row - out_row
                        valid = abs(dr) <= 1
                        dw = par - out_par
                        if blk == 1:
                            valid = valid and dw != 0
                            dw = -dw
                        at = (dt * 2 + blk) * lanes + g * lat
                        tap = ((2 - dt) * 3 + dr + 1) * 3 + dw + 1
                        wst_ref[row * 2 + par, at : at + lat, :] = (
                            w_ref[tap * lat : (tap + 1) * lat, :]
                            if valid
                            else jnp.zeros((lat, ch), BF16)
                        )
    loads[1].wait()
    raw = feat_ref[...].astype(F32)
    act = raw / (1.0 + jnp.exp(-raw))
    for i in range(ch // 128):
        act_ref[i] = act[:, i * 128 : (i + 1) * 128]
    half = fr * 2 * cols
    total = None
    for par in range(2):
        mine = jnp.concatenate(
            [
                act_ref[i, pl.ds(par, half, stride=2), :].astype(BF16)
                for i in range(ch // 128)
            ],
            axis=1,
        ).reshape(fr, 2, cols, ch)
        for row in range(2):
            term = lax.dot_general(
                mine[:, row].reshape(fr * cols, ch),
                wst_ref[row * 2 + par],
                NT,
                preferred_element_type=F32,
            )
            total = term if total is None else total + term
    loads[2].wait()
    starts = [jnp.int32(0)] * (fr + 2)
    begin = jnp.int32(0)
    for c in range(clips):
        end = begin + frames_ref[c]
        for f in range(fr + 2):
            t = slab * fr + f
            starts[f] = jnp.where((t >= begin) & (t < end), begin, starts[f])
        begin = end
    sums = []
    for blk in range(2):
        pieces = []
        for f in range(fr + 2):
            piece = jnp.zeros((cols, lanes), F32)
            for dt in range(3):
                src = f - dt
                if 0 <= src < fr:
                    keep = (slab * fr + src >= starts[f]).astype(F32)
                    at = (dt * 2 + blk) * lanes
                    piece = piece + keep * total[src * cols : (src + 1) * cols, at : at + lanes]
            pieces.append(piece)
        sums.append(jnp.concatenate(pieces, axis=0))
    same, side = sums
    rows = (fr + 2) * cols
    col_at = lax.broadcasted_iota(jnp.int32, (rows, lanes), 0) % cols
    par_at = (lax.broadcasted_iota(jnp.int32, (rows, lanes), 1) // lat) % 2
    after = jnp.where(col_at < cols - 1, pltpu.roll(side, rows - 1, 0), 0.0)
    before = jnp.where(col_at > 0, pltpu.roll(side, 1, 0), 0.0)
    part_ref[...] = (same + jnp.where(par_at == 1, after, before)).astype(BF16)


def table_kernel(dims, after_ref, frames_hbm, group_hbm, offset_hbm, times_hbm, noise_hbm, *rest):
    fr, cols, clips, n_dp, patch, width = dims
    pick_ref, scale_ref, noise_ref, live_ref, mark_ref = rest[:5]
    frames_ref, group_ref, offset_ref, times_ref, raw_ref, sems = rest[5:]
    loads = [
        pltpu.make_async_copy(source, target, sems.at[i])
        for i, (source, target) in enumerate(
            (
                (frames_hbm, frames_ref),
                (group_hbm, group_ref),
                (offset_hbm, offset_ref),
                (times_hbm, times_ref),
                (noise_hbm, raw_ref),
            )
        )
    ]
    for load in loads:
        load.start()
    for load in loads:
        load.wait()
    slab = lax.axis_index("dp")
    source = [jnp.int32(-1)] * fr
    owner = [jnp.int32(clips)] * fr
    level = [jnp.float32(0.0)] * fr
    usable = [jnp.float32(0.0)] * fr
    begin = jnp.int32(0)
    for c in range(clips):
        size, off = frames_ref[c], offset_ref[c]
        here = group_ref[c] == slab
        for f in range(fr):
            member = here & (off <= f) & (f < off + size)
            source[f] = jnp.where(member, begin + f - off, source[f])
            owner[f] = jnp.where(member, c, owner[f])
            usable[f] = jnp.where(member, 1.0, usable[f])
            level[f] = jnp.where(member, times_ref[c], level[f])
        begin = begin + size
    rows = (fr + 2) * cols
    noise = raw_ref[...].astype(F32).T
    noise = jnp.concatenate([noise, jnp.zeros((fr * cols, width - patch), F32)], axis=1)
    ahead = lax.broadcasted_iota(jnp.int32, (cols, n_dp * rows), 1) - lax.broadcasted_iota(
        jnp.int32, (cols, n_dp * rows), 0
    )
    lane = lax.broadcasted_iota(jnp.int32, (cols, width), 1)
    for f in range(fr):
        here = slice(f * cols, (f + 1) * cols)
        hit = None
        for m in range(n_dp):
            at = source[f] - (slab ^ m) * fr
            valid = (at >= 0) & (at < fr + 2) & (source[f] >= 0)
            at = jnp.where(valid, m * rows + at * cols, -cols)
            hit = (ahead == at) if hit is None else hit | (ahead == at)
        pick_ref[here, :] = hit.astype(F32).astype(BF16)
        scale_ref[here, :] = jnp.full((cols, width), usable[f] * (1.0 - level[f]), F32)
        noise_ref[here, :] = (usable[f] * level[f]) * noise[here]
        live_ref[here, :] = jnp.full((cols, width), usable[f], F32)
        mark_ref[here, :] = (lane == owner[f]).astype(F32)


def slot_kernel(dims, pick_ref, scale_ref, noise_ref, *rest):
    (n_dp,) = dims
    part_refs, (send_ref, own_ref) = rest[:n_dp], rest[n_dp:]
    parts = jnp.concatenate([ref[...] for ref in part_refs], axis=0)
    got = jnp.dot(pick_ref[...], parts, preferred_element_type=F32)
    own = scale_ref[...] * got + noise_ref[...]
    own_ref[...] = own
    send_ref[...] = own.astype(BF16)


def weight_kernel(dims, after_ref, embed_hbm, proj_hbm, gains_hbm, out_ref, gains_ref, *rest):
    patch, head = dims
    embed_ref, proj_ref, sems = rest
    loads = [
        pltpu.make_async_copy(embed_hbm, embed_ref, sems.at[0]),
        pltpu.make_async_copy(gains_hbm, gains_ref, sems.at[1]),
    ] + [pltpu.make_async_copy(proj_hbm.at[i], proj_ref.at[i], sems.at[2 + i]) for i in range(3)]
    for load in loads:
        load.start()
    loads[0].wait()
    for i in range(3):
        loads[2 + i].wait()
        both = jnp.dot(embed_ref[...], proj_ref[i], preferred_element_type=F32).astype(BF16)
        at = slice(i * head, (i + 1) * head)
        out_ref[:patch, at] = both
        out_ref[patch : 3 * patch, at] = jnp.zeros((2 * patch, head), BF16)
        out_ref[3 * patch :, at] = both
    loads[1].wait()


def mean_of(values):
    return jnp.mean(values, axis=-1, keepdims=True)


def chunk_of(size):
    return min(size, 512)


def attention_kernel(dims, gains_ref, w_ref, own_ref, live_ref, mark_ref, *rest):
    fr, cols, n_seq, patch, head, tile = dims
    tok_refs, cot_refs, rest = rest[:n_seq], rest[n_seq : 2 * n_seq], rest[2 * n_seq :]
    noisy_ref, grad_ref = rest[:2]
    pairs_refs, rest = rest[2 : 2 + n_seq // 2], rest[2 + n_seq // 2 :]
    tok_ref, inc_ref, cat_ref, unit_ref, scale_ref, q_ref, k_ref, v_ref, o_ref, dq_ref, dk_ref, dv_ref = rest
    me = lax.axis_index("seq")
    blk = fr * cols
    size = n_seq * blk
    width = 2 * patch
    tok_ref[:blk, :] = jnp.zeros((blk, width), BF16)
    tok_ref[size + blk :, :] = jnp.zeros((blk, width), BF16)
    for m in range(n_seq):
        at = pl.multiple_of((me ^ m) * blk, blk)
        tok_ref[pl.ds(at + blk, blk), :] = tok_refs[m][...]
        inc_ref[pl.ds(at, blk), :] = cot_refs[m // 2 + (m % 2) * (n_seq // 2)][m % 2]
    own_at = pl.multiple_of(me * blk, blk)
    lane = lax.broadcasted_iota(jnp.int32, (blk, width), 1)
    side = jnp.where(
        lane < patch + patch // 2,
        tok_ref[pl.ds(own_at, blk), :].astype(F32),
        tok_ref[pl.ds(own_at + 2 * blk, blk), :].astype(F32),
    )
    noisy = own_ref[...] + pltpu.roll(side, patch, 1)
    noisy_ref[...] = noisy.T[:patch, :]
    marks = jnp.concatenate([mark_ref[...].astype(BF16)] * (chunk_of(size) // blk), axis=0)
    away = ((marks.astype(F32) - 1.0) * BIG).astype(BF16)
    weights = w_ref[...]
    chunk = chunk_of(size)
    lane = lax.broadcasted_iota(jnp.int32, (chunk, width), 1)
    for p in range(size // chunk):
        at = p * chunk
        rows = slice(at, at + chunk)
        cat_ref[rows, :width] = tok_ref[at + blk : at + blk + chunk, :]
        cat_ref[rows, width:] = jnp.where(
            lane < patch + patch // 2,
            tok_ref[rows, :].astype(F32),
            tok_ref[at + 2 * blk : at + 2 * blk + chunk, :].astype(F32),
        ).astype(BF16)
        x = jnp.dot(cat_ref[rows, :], weights, preferred_element_type=F32)
        v_ref[rows, :head] = x[:, 2 * head :].astype(BF16)
        v_ref[rows, head:] = jnp.ones((chunk, head), BF16)
        for i, ref in enumerate((q_ref, k_ref)):
            mine = x[:, i * head : (i + 1) * head]
            scale = jnp.broadcast_to(lax.rsqrt(mean_of(mine * mine) + EPS), mine.shape)
            unit = mine * scale
            unit_ref[rows, i * head : (i + 1) * head] = unit
            scale_ref[rows, i * head : (i + 1) * head] = scale
            gain = gains_ref[i : i + 1, :] * (1.0 if i else head**-0.5 * LOG2E)
            ref[rows, :head] = (unit * gain).astype(BF16)
        q_ref[rows, head:] = marks
        k_ref[rows, head:] = away
    per = tile // blk
    live = jnp.concatenate([live_ref[...]] * per, axis=0)
    for i in range(size // tile):
        rows = slice(i * tile, (i + 1) * tile)
        scores = lax.dot_general(q_ref[rows, :], k_ref[...], NT, preferred_element_type=F32)
        exps = jnp.exp2(scores)
        exps_bf = exps.astype(BF16)
        both = jnp.dot(exps_bf, v_ref[...], preferred_element_type=F32)
        inverse = 1.0 / both[:, head:]
        output = both[:, :head] * inverse
        o_ref[rows, :] = (output * live).astype(BF16)
        scaled = inc_ref[rows, :].astype(F32) * live * inverse
        scaled_bf = scaled.astype(BF16)
        upstream = jnp.concatenate([scaled_bf, (-(scaled * output)).astype(BF16)], axis=1)
        prob_grad = lax.dot_general(upstream, v_ref[...], NT, preferred_element_type=F32)
        score_grad = (exps * prob_grad).astype(BF16)
        dq_ref[rows, :] = jnp.dot(score_grad, k_ref[:, :head], preferred_element_type=F32)
        dk = lax.dot_general(score_grad, q_ref[rows, :head], TN, preferred_element_type=F32)
        dv = lax.dot_general(exps_bf, scaled_bf, TN, preferred_element_type=F32)
        if i == 0:
            dk_ref[...] = dk
            dv_ref[...] = dv
        else:
            dk_ref[...] += dk
            dv_ref[...] += dv

    gains = [None, None]
    grad = None
    for p in range(size // chunk):
        rows = slice(p * chunk, (p + 1) * chunk)
        parts = []
        for i, (ref, unit) in enumerate(((dq_ref, head**-0.5), (dk_ref, 1.0 / LOG2E))):
            mine = unit_ref[rows, i * head : (i + 1) * head]
            up = ref[rows, :] * unit
            gain_up = up * gains_ref[i : i + 1, :]
            scale = scale_ref[rows, i * head : (i + 1) * head]
            parts.append((scale * (gain_up - mine * mean_of(mine * gain_up))).astype(BF16))
            add = jnp.sum(up * mine, axis=0, keepdims=True)
            gains[i] = add if p == 0 else gains[i] + add
        parts.append(dv_ref[rows, :].astype(BF16))
        term = lax.dot_general(
            cat_ref[rows, :], jnp.concatenate(parts, axis=1), TN, preferred_element_type=F32
        )
        grad = term if grad is None else grad + term
    grad_ref[:patch, :] = (grad[:patch, :] + grad[3 * patch :, :]).astype(BF16)
    sums = jnp.concatenate(gains + [jnp.zeros((1, head), F32)], axis=1)
    high = sums.astype(BF16).astype(F32)
    grad_ref[patch:, :] = jnp.concatenate(
        [high, sums - high, jnp.zeros((EXTRA - 2, 3 * head), F32)], axis=0
    ).astype(BF16)
    for m in range(n_seq):
        at = pl.multiple_of((me ^ m) * blk, blk)
        pairs_refs[m // 2][m % 2] = o_ref[pl.ds(at, blk), :]


def proj_kernel(dims, embed_ref, *rest):
    n_dp, patch, head, rows = dims
    grad_refs, (out_ref,) = rest[:n_dp], rest[n_dp:]
    slab = lax.axis_index("dp")
    part = embed_ref[:, pl.ds(pl.multiple_of(slab * rows, rows), rows)]
    left = jnp.concatenate([part] * n_dp, axis=0)
    right = jnp.concatenate([ref[:patch, :] for ref in grad_refs], axis=0)
    result = lax.dot_general(left, right, TN, preferred_element_type=F32)
    for i in range(3):
        out_ref[pl.ds(i, rows, stride=3), :] = result[:, i * head : (i + 1) * head]


def group_sum_kernel(dims, *rest):
    n_dp, patch, head = dims
    grad_refs, (out_ref, all_ref) = rest[:n_dp], rest[n_dp:]
    slab = lax.axis_index("dp")
    for m in range(n_dp):
        all_ref[slab ^ m] = grad_refs[m][patch:, :].astype(F32)
    total = all_ref[0]
    for g in range(1, n_dp):
        total = total + all_ref[g]
    both = total[0:1, :] + total[1:2, :]
    out_ref[...] = jnp.concatenate(
        [both[:, :head], both[:, head : 2 * head], jnp.zeros((6, head), F32)], axis=0
    )


def chip_sum_kernel(dims, *rest):
    (half,) = dims
    sum_refs, (out_ref, all_ref) = rest[:half], rest[half:]
    chip = lax.axis_index("seq") // 2
    for m in range(half):
        all_ref[chip ^ m] = sum_refs[m][...]
    total = all_ref[0]
    for z in range(1, half):
        total = total + all_ref[z]
    out_ref[...] = total


def finish_kernel(dims, sum_ref, other_ref, *rest):
    n_seq, head = dims
    pair_refs, (out_ref, gain_ref) = rest[:n_seq], rest[n_seq:]
    me = lax.axis_index("seq")
    for m in range(n_seq):
        at = pl.multiple_of((me ^ m) * head, head)
        out_ref[:, pl.ds(at, head)] = pair_refs[m // 2 + (m % 2) * (n_seq // 2)][m % 2]
    gain_ref[...] = sum_ref[0:2, :] + other_ref[0:2, :]


def body(
    features,
    conv_weight,
    clip_frames,
    clip_group,
    clip_offset,
    clip_times,
    noise_tokens,
    embed_weight,
    attention_proj,
    norm_gains,
    cotangent,
):
    n_dp, n_seq = lax.axis_size("dp"), lax.axis_size("seq")
    fr, rows_dev, wd, ch = features.shape
    lat = conv_weight.shape[3]
    clips = clip_frames.shape[0]
    cols = wd // 2
    blk, patch = noise_tokens.shape[1:]
    model, _, heads_dev, head = attention_proj.shape
    assert rows_dev == 2 and heads_dev == 1 and blk == fr * cols and patch == 4 * lat
    size = n_seq * blk
    lanes = len(CELLS) * lat
    S = jax.ShapeDtypeStruct

    rows_out = (fr + 2) * cols
    tile = min(512, size)

    half = n_seq // 2
    cots = pl.pallas_call(
        functools.partial(split_kernel, (n_seq, head)),
        out_shape=[S((2, blk, head), BF16)] * half,
        in_specs=[HBM],
        out_specs=[VMEM] * half,
        scratch_shapes=[pltpu.SemaphoreType.DMA((n_seq,))],
        compiler_params=params(),
        cost_estimate=cost(0, 4 * blk * n_seq * head),
        name="split",
    )(*keep_in(pltpu.HBM, cotangent.reshape(blk, n_seq * head)))
    cots = [cots[0]] + [swap(cots[m], "seq", 2 * m) for m in range(1, half)]
    cots += [swap(pair, "seq", 1) for pair in cots]

    partial = pl.pallas_call(
        functools.partial(conv_kernel, (fr, wd, ch, lat, clips)),
        out_shape=S((rows_out, lanes), BF16),
        in_specs=[HBM] * 3,
        out_specs=VMEM,
        scratch_shapes=[
            pltpu.SMEM((clips,), jnp.int32),
            pltpu.VMEM((fr * 2 * wd, ch), BF16),
            pltpu.VMEM((27 * lat, ch), BF16),
            pltpu.VMEM((ch // 128, fr * 2 * wd, 128), F32),
            pltpu.VMEM((4, 6 * lanes, ch), BF16),
            pltpu.SemaphoreType.DMA((3,)),
        ],
        compiler_params=params(),
        cost_estimate=cost(2 * fr * cols * 4 * ch * 6 * lanes, 2**21, fr * 2 * wd * ch),
        name="conv",
    )(
        *keep_in(
            pltpu.HBM,
            clip_frames,
            features.reshape(fr * 2 * wd, ch),
            conv_weight.reshape(27 * lat, ch),
        )
    )
    parts = [partial] + [swap(partial, "dp", m) for m in range(1, n_dp)]
    pick, scale, noise, live, mark = pl.pallas_call(
        functools.partial(table_kernel, (fr, cols, clips, n_dp, patch, lanes)),
        out_shape=[S((blk, n_dp * rows_out), BF16)] + [S((blk, lanes), F32)] * 4,
        in_specs=[VMEM] + [HBM] * 5,
        out_specs=[VMEM] * 5,
        scratch_shapes=[pltpu.SMEM((clips,), jnp.int32)] * 3
        + [
            pltpu.SMEM((clips,), F32),
            pltpu.VMEM((patch, blk), BF16),
            pltpu.SemaphoreType.DMA((5,)),
        ],
        compiler_params=params(),
        cost_estimate=cost(2**22, 2**21),
        name="tables",
    )(partial, clip_frames, clip_group, clip_offset, clip_times, noise_tokens[0].T)

    send, own = pl.pallas_call(
        functools.partial(slot_kernel, (n_dp,)),
        out_shape=[S((blk, lanes), BF16), S((blk, lanes), F32)],
        in_specs=[VMEM] * (3 + n_dp),
        out_specs=[VMEM] * 2,
        compiler_params=params(),
        cost_estimate=cost(2**20, 2**18),
        name="slots",
    )(pick, scale, noise, *parts)
    toks = [send] + [None] * (n_seq - 1)
    for m in range(2, n_seq, 2):
        toks[m] = swap(send, "seq", m)
    for m in range(0, n_seq, 2):
        toks[m + 1] = swap(toks[m], "seq", 1)
    weights, gains = pl.pallas_call(
        functools.partial(weight_kernel, (patch, head)),
        out_shape=[S((4 * patch, 3 * head), BF16), S((2, head), F32)],
        in_specs=[VMEM] + [HBM] * 3,
        out_specs=[VMEM] * 2,
        scratch_shapes=[
            pltpu.VMEM((patch, model), BF16),
            pltpu.VMEM((3, model, head), BF16),
            pltpu.SemaphoreType.DMA((5,)),
        ],
        compiler_params=params(),
        cost_estimate=cost(2 * patch * model * 3 * head, 2 * model * (3 * head + patch)),
        name="weights",
    )(send, embed_weight, attention_proj.transpose(1, 2, 0, 3).reshape(3, model, head), norm_gains)

    wide = 2 * head
    noisy, grad, *pairs = pl.pallas_call(
        functools.partial(attention_kernel, (fr, cols, n_seq, patch, head, tile)),
        out_shape=[S((patch, blk), F32), S((patch + EXTRA, 3 * head), BF16)]
        + [S((2, blk, head), BF16)] * half,
        in_specs=[VMEM] * (5 + 2 * n_seq),
        out_specs=[VMEM] * (2 + half),
        scratch_shapes=[
            pltpu.VMEM((size + 2 * blk, lanes), BF16),
            pltpu.VMEM((size, head), BF16),
            pltpu.VMEM((size, 2 * lanes), BF16),
            pltpu.VMEM((size, wide), F32),
            pltpu.VMEM((size, wide), F32),
            pltpu.VMEM((size, wide), BF16),
            pltpu.VMEM((size, wide), BF16),
            pltpu.VMEM((size, wide), BF16),
            pltpu.VMEM((size, head), BF16),
            pltpu.VMEM((size, head), F32),
            pltpu.VMEM((size, head), F32),
            pltpu.VMEM((size, head), F32),
        ],
        compiler_params=params(),
        cost_estimate=cost(12 * size * size * head, 2**21, size * size),
        name="attention",
    )(gains, weights, own, live, mark, *toks, *cots)

    pairs = [pairs[0]] + [swap(pairs[m], "seq", 2 * m) for m in range(1, half)]
    grads = [grad] + [swap(grad, "dp", m) for m in range(1, n_dp)]
    gain = pl.pallas_call(
        functools.partial(group_sum_kernel, (n_dp, patch, head)),
        out_shape=S((8, head), F32),
        in_specs=[VMEM] * n_dp,
        out_specs=VMEM,
        scratch_shapes=[pltpu.VMEM((n_dp, EXTRA, 3 * head), F32)],
        compiler_params=params(),
        cost_estimate=cost(0, 2**12),
        name="groupsum",
    )(*grads)
    gain = [gain] + [swap(gain, "seq", 2 * m) for m in range(1, half)]
    gain = pl.pallas_call(
        functools.partial(chip_sum_kernel, (half,)),
        out_shape=S((8, head), F32),
        in_specs=[VMEM] * half,
        out_specs=VMEM,
        scratch_shapes=[pltpu.VMEM((half, 8, head), F32)],
        compiler_params=params(),
        cost_estimate=cost(0, 2**12),
        name="chipsum",
    )(*gain)
    other = swap(gain, "seq", 1)
    pairs += [swap(pair, "seq", 1) for pair in pairs]
    rows = model // n_dp
    proj_grad = pl.pallas_call(
        functools.partial(proj_kernel, (n_dp, patch, head, rows)),
        out_shape=S((rows * 3, head), F32),
        in_specs=[VMEM] * (1 + n_dp),
        out_specs=VMEM,
        compiler_params=params(),
        cost_estimate=cost(2 * rows * 3 * head * patch * n_dp, 4 * rows * 3 * head),
        name="projgrad",
    )(embed_weight, *grads)
    out, norm_grad = pl.pallas_call(
        functools.partial(finish_kernel, (n_seq, head)),
        out_shape=[S((blk, n_seq * head), BF16), S((2, head), F32)],
        in_specs=[VMEM] * (2 + n_seq),
        out_specs=[VMEM] * 2,
        compiler_params=params(),
        cost_estimate=cost(0, 4 * blk * n_seq * head),
        name="finish",
    )(gain, other, *pairs)
    return (
        noisy.T[None],
        out[None],
        proj_grad.reshape(rows, 3, heads_dev, head),
        norm_grad,
    )


def solution(mesh):
    return jax.shard_map(
        body,
        mesh=mesh,
        in_specs=(
            P("dp", "seq", None, None),
            P(),
            P(),
            P(),
            P(),
            P(),
            P("dp", "seq", None),
            P(),
            P(None, None, "seq", None),
            P(),
            P("dp", "seq", None),
        ),
        out_specs=(P("dp", "seq", None), P("dp", "seq", None), P("dp", None, "seq", None), P()),
        check_vma=False,
    )
```

```python
import functools

import jax
import jax.numpy as jnp
from jax import lax
from jax.experimental import pallas as pl
from jax.experimental.pallas import tpu as pltpu
from jax.sharding import PartitionSpec as P


F32 = jnp.float32
BF16 = jnp.bfloat16
LOG2E = 1.4426950408889634
EPS = 1e-06
BIG = 16384.0
EXTRA = 16
CELLS = ((0, 0), (0, 1), (1, 0), (1, 1), (2, 0), (2, 1), (-1, 0), (-1, 1))
NT = (((1,), (1,)), ((), ()))
TN = (((0,), (0,)), ((), ()))


def swap(block, axis, mask):
    return lax.ppermute(block, axis, [(i, i ^ mask) for i in range(lax.axis_size(axis))])


def keep_in(space, *arrays):
    return [pltpu.with_memory_space_constraint(a, space) for a in arrays]


def cost(flops, moved, exps=0):
    return pl.CostEstimate(flops=int(flops), bytes_accessed=int(moved), transcendentals=int(exps))


def params(mib=48):
    return pltpu.CompilerParams(vmem_limit_bytes=mib * 1024 * 1024)


VMEM = pl.BlockSpec(memory_space=pltpu.VMEM)
SMEM = pl.BlockSpec(memory_space=pltpu.SMEM)
HBM = pl.BlockSpec(memory_space=pltpu.HBM)


def split_kernel(dims, after_ref, cot_ref, *pair_refs):
    n_seq, head = dims
    me = lax.axis_index("seq")
    for m in range(n_seq):
        at = pl.multiple_of((me ^ m) * head, head)
        pair_refs[m // 2][m % 2] = cot_ref[:, pl.ds(at, head)]


def conv_kernel(dims, frames_hbm, feat_hbm, w_hbm, part_ref, *rest):
    fr, wd, ch, lat, clips = dims
    frames_ref, feat_ref, w_ref, act_ref, wst_ref, sems = rest
    cols = wd // 2
    slab = lax.axis_index("dp")
    loads = [
        pltpu.make_async_copy(w_hbm, w_ref, sems.at[0]),
        pltpu.make_async_copy(feat_hbm, feat_ref, sems.at[1]),
        pltpu.make_async_copy(frames_hbm, frames_ref, sems.at[2]),
    ]
    for load in loads:
        load.start()
    loads[0].wait()
    lanes = len(CELLS) * lat
    for row in range(2):
        for par in range(2):
            for dt in range(3):
                for blk in range(2):
                    for g, (out_row, out_par) in enumerate(CELLS):
                        dr = row - out_row
                        valid = abs(dr) <= 1
                        dw = par - out_par
                        if blk == 1:
                            valid = valid and dw != 0
                            dw = -dw
                        at = (dt * 2 + blk) * lanes + g * lat
                        tap = ((2 - dt) * 3 + dr + 1) * 3 + dw + 1
                        wst_ref[row * 2 + par, at : at + lat, :] = (
                            w_ref[tap * lat : (tap + 1) * lat, :]
                            if valid
                            else jnp.zeros((lat, ch), BF16)
                        )
    loads[1].wait()
    raw = feat_ref[...].astype(F32)
    act = raw / (1.0 + jnp.exp(-raw))
    for i in range(ch // 128):
        act_ref[i] = act[:, i * 128 : (i + 1) * 128]
    half = fr * 2 * cols
    total = None
    for par in range(2):
        mine = jnp.concatenate(
            [
                act_ref[i, pl.ds(par, half, stride=2), :].astype(BF16)
                for i in range(ch // 128)
            ],
            axis=1,
        ).reshape(fr, 2, cols, ch)
        for row in range(2):
            term = lax.dot_general(
                mine[:, row].reshape(fr * cols, ch),
                wst_ref[row * 2 + par],
                NT,
                preferred_element_type=F32,
            )
            total = term if total is None else total + term
    loads[2].wait()
    starts = [jnp.int32(0)] * (fr + 2)
    begin = jnp.int32(0)
    for c in range(clips):
        end = begin + frames_ref[c]
        for f in range(fr + 2):
            t = slab * fr + f
            starts[f] = jnp.where((t >= begin) & (t < end), begin, starts[f])
        begin = end
    sums = []
    for blk in range(2):
        pieces = []
        for f in range(fr + 2):
            piece = jnp.zeros((cols, lanes), F32)
            for dt in range(3):
                src = f - dt
                if 0 <= src < fr:
                    keep = (slab * fr + src >= starts[f]).astype(F32)
                    at = (dt * 2 + blk) * lanes
                    piece = piece + keep * total[src * cols : (src + 1) * cols, at : at + lanes]
            pieces.append(piece)
        sums.append(jnp.concatenate(pieces, axis=0))
    same, side = sums
    rows = (fr + 2) * cols
    col_at = lax.broadcasted_iota(jnp.int32, (rows, lanes), 0) % cols
    par_at = (lax.broadcasted_iota(jnp.int32, (rows, lanes), 1) // lat) % 2
    after = jnp.where(col_at < cols - 1, pltpu.roll(side, rows - 1, 0), 0.0)
    before = jnp.where(col_at > 0, pltpu.roll(side, 1, 0), 0.0)
    part_ref[...] = (same + jnp.where(par_at == 1, after, before)).astype(BF16)


def table_kernel(dims, frames_ref, group_ref, offset_ref, times_ref, after_ref, raw_ref, *rest):
    fr, cols, clips, n_dp, patch, width = dims
    pick_ref, scale_ref, noise_ref, live_ref, mark_ref = rest
    slab = lax.axis_index("dp")
    source = [jnp.int32(-1)] * fr
    owner = [jnp.int32(clips)] * fr
    level = [jnp.float32(0.0)] * fr
    usable = [jnp.float32(0.0)] * fr
    begin = jnp.int32(0)
    for c in range(clips):
        size, off = frames_ref[c], offset_ref[c]
        here = group_ref[c] == slab
        for f in range(fr):
            member = here & (off <= f) & (f < off + size)
            source[f] = jnp.where(member, begin + f - off, source[f])
            owner[f] = jnp.where(member, c, owner[f])
            usable[f] = jnp.where(member, 1.0, usable[f])
            level[f] = jnp.where(member, times_ref[c], level[f])
        begin = begin + size
    rows = (fr + 2) * cols
    noise = raw_ref[...].astype(F32).T
    noise = jnp.concatenate([noise, jnp.zeros((fr * cols, width - patch), F32)], axis=1)
    ahead = lax.broadcasted_iota(jnp.int32, (cols, n_dp * rows), 1) - lax.broadcasted_iota(
        jnp.int32, (cols, n_dp * rows), 0
    )
    lane = lax.broadcasted_iota(jnp.int32, (cols, width), 1)
    for f in range(fr):
        here = slice(f * cols, (f + 1) * cols)
        hit = None
        for m in range(n_dp):
            at = source[f] - (slab ^ m) * fr
            valid = (at >= 0) & (at < fr + 2) & (source[f] >= 0)
            at = jnp.where(valid, m * rows + at * cols, -cols)
            hit = (ahead == at) if hit is None else hit | (ahead == at)
        pick_ref[here, :] = hit.astype(F32).astype(BF16)
        scale_ref[here, :] = jnp.full((cols, width), usable[f] * (1.0 - level[f]), F32)
        noise_ref[here, :] = (usable[f] * level[f]) * noise[here]
        live_ref[here, :] = jnp.full((cols, width), usable[f], F32)
        mark_ref[here, :] = (lane == owner[f]).astype(F32)


def slot_kernel(dims, pick_ref, scale_ref, noise_ref, *rest):
    (n_dp,) = dims
    part_refs, (send_ref, own_ref) = rest[:n_dp], rest[n_dp:]
    parts = jnp.concatenate([ref[...] for ref in part_refs], axis=0)
    got = jnp.dot(pick_ref[...], parts, preferred_element_type=F32)
    own = scale_ref[...] * got + noise_ref[...]
    own_ref[...] = own
    send_ref[...] = own.astype(BF16)


def weight_kernel(dims, after_ref, embed_ref, proj_ref, out_ref):
    patch, head = dims
    for i in range(3):
        both = jnp.dot(embed_ref[...], proj_ref[i], preferred_element_type=F32).astype(BF16)
        at = slice(i * head, (i + 1) * head)
        out_ref[:patch, at] = both
        out_ref[patch : 3 * patch, at] = jnp.zeros((2 * patch, head), BF16)
        out_ref[3 * patch :, at] = both


def mean_of(values):
    return jnp.mean(values, axis=-1, keepdims=True)


def chunk_of(size):
    return min(size, 512)


def attention_kernel(dims, gains_ref, w_ref, own_ref, live_ref, mark_ref, *rest):
    fr, cols, n_seq, patch, head, tile = dims
    tok_refs, cot_refs, rest = rest[:n_seq], rest[n_seq : 2 * n_seq], rest[2 * n_seq :]
    noisy_ref, grad_ref = rest[:2]
    pair_refs, rest = rest[2 : 2 + n_seq // 2], rest[2 + n_seq // 2 :]
    tok_ref, inc_ref, cat_ref, unit_ref, scale_ref = rest[:5]
    q_ref, k_ref, v_ref, o_ref, dq_ref, dk_ref, dv_ref = rest[5:]
    me = lax.axis_index("seq")
    blk = fr * cols
    size = n_seq * blk
    width = 2 * patch
    tok_ref[:blk, :] = jnp.zeros((blk, width), BF16)
    tok_ref[size + blk :, :] = jnp.zeros((blk, width), BF16)
    for m in range(n_seq):
        at = pl.multiple_of((me ^ m) * blk, blk)
        tok_ref[pl.ds(at + blk, blk), :] = tok_refs[m][...]
        inc_ref[pl.ds(at, blk), :] = cot_refs[m // 2 + (m % 2) * (n_seq // 2)][m % 2]
    own_at = pl.multiple_of(me * blk, blk)
    lane = lax.broadcasted_iota(jnp.int32, (blk, width), 1)
    side = jnp.where(
        lane < patch + patch // 2,
        tok_ref[pl.ds(own_at, blk), :].astype(F32),
        tok_ref[pl.ds(own_at + 2 * blk, blk), :].astype(F32),
    )
    noisy = own_ref[...] + pltpu.roll(side, patch, 1)
    noisy_ref[...] = noisy.T[:patch, :]
    marks = jnp.concatenate([mark_ref[...].astype(BF16)] * (chunk_of(size) // blk), axis=0)
    away = ((marks.astype(F32) - 1.0) * BIG).astype(BF16)
    weights = w_ref[...]
    chunk = chunk_of(size)
    lane = lax.broadcasted_iota(jnp.int32, (chunk, width), 1)
    for p in range(size // chunk):
        at = p * chunk
        rows = slice(at, at + chunk)
        cat_ref[rows, :width] = tok_ref[at + blk : at + blk + chunk, :]
        cat_ref[rows, width:] = jnp.where(
            lane < patch + patch // 2,
            tok_ref[rows, :].astype(F32),
            tok_ref[at + 2 * blk : at + 2 * blk + chunk, :].astype(F32),
        ).astype(BF16)
        x = jnp.dot(cat_ref[rows, :], weights, preferred_element_type=F32)
        v_ref[rows, :head] = x[:, 2 * head :].astype(BF16)
        v_ref[rows, head:] = jnp.ones((chunk, head), BF16)
        for i, ref in enumerate((q_ref, k_ref)):
            mine = x[:, i * head : (i + 1) * head]
            scale = jnp.broadcast_to(lax.rsqrt(mean_of(mine * mine) + EPS), mine.shape)
            unit = mine * scale
            unit_ref[rows, i * head : (i + 1) * head] = unit
            scale_ref[rows, i * head : (i + 1) * head] = scale
            gain = gains_ref[i : i + 1, :] * (1.0 if i else head**-0.5 * LOG2E)
            ref[rows, :head] = (unit * gain).astype(BF16)
        q_ref[rows, head:] = marks
        k_ref[rows, head:] = away
    per = tile // blk
    live = jnp.concatenate([live_ref[...]] * per, axis=0)
    for i in range(size // tile):
        rows = slice(i * tile, (i + 1) * tile)
        scores = lax.dot_general(q_ref[rows, :], k_ref[...], NT, preferred_element_type=F32)
        exps = jnp.exp2(scores)
        exps_bf = exps.astype(BF16)
        both = jnp.dot(exps_bf, v_ref[...], preferred_element_type=F32)
        inverse = 1.0 / both[:, head:]
        output = both[:, :head] * inverse
        o_ref[rows, :] = (output * live).astype(BF16)
        scaled = inc_ref[rows, :].astype(F32) * live * inverse
        scaled_bf = scaled.astype(BF16)
        upstream = jnp.concatenate([scaled_bf, (-(scaled * output)).astype(BF16)], axis=1)
        prob_grad = lax.dot_general(upstream, v_ref[...], NT, preferred_element_type=F32)
        score_grad = (exps * prob_grad).astype(BF16)
        dq_ref[rows, :] = jnp.dot(score_grad, k_ref[:, :head], preferred_element_type=F32)
        dk = lax.dot_general(score_grad, q_ref[rows, :head], TN, preferred_element_type=F32)
        dv = lax.dot_general(exps_bf, scaled_bf, TN, preferred_element_type=F32)
        if i == 0:
            dk_ref[...] = dk
            dv_ref[...] = dv
        else:
            dk_ref[...] += dk
            dv_ref[...] += dv

    gains = [None, None]
    grad = None
    for p in range(size // chunk):
        rows = slice(p * chunk, (p + 1) * chunk)
        parts = []
        for i, (ref, unit) in enumerate(((dq_ref, head**-0.5), (dk_ref, 1.0 / LOG2E))):
            mine = unit_ref[rows, i * head : (i + 1) * head]
            up = ref[rows, :] * unit
            gain_up = up * gains_ref[i : i + 1, :]
            scale = scale_ref[rows, i * head : (i + 1) * head]
            parts.append((scale * (gain_up - mine * mean_of(mine * gain_up))).astype(BF16))
            add = jnp.sum(up * mine, axis=0, keepdims=True)
            gains[i] = add if p == 0 else gains[i] + add
        parts.append(dv_ref[rows, :].astype(BF16))
        term = lax.dot_general(
            cat_ref[rows, :], jnp.concatenate(parts, axis=1), TN, preferred_element_type=F32
        )
        grad = term if grad is None else grad + term
    grad_ref[...] = (grad[:patch, :] + grad[3 * patch :, :]).astype(BF16)
    sums = jnp.concatenate(gains, axis=0)
    high = sums.astype(BF16).astype(F32)
    block = jnp.concatenate([high, sums - high, jnp.zeros((EXTRA - 4, head), F32)], axis=0)
    for m in range(n_seq):
        at = pl.multiple_of((me ^ m) * blk, blk)
        pair_refs[m // 2][m % 2, :blk] = o_ref[pl.ds(at, blk), :]
        pair_refs[m // 2][m % 2, blk:] = block.astype(BF16)


def proj_kernel(dims, embed_ref, *rest):
    n_dp, _, head, rows = dims
    grad_refs, (out_ref,) = rest[:n_dp], rest[n_dp:]
    slab = lax.axis_index("dp")
    part = embed_ref[:, pl.ds(pl.multiple_of(slab * rows, rows), rows)]
    left = jnp.concatenate([part] * n_dp, axis=0)
    right = jnp.concatenate([ref[...] for ref in grad_refs], axis=0)
    result = lax.dot_general(left, right, TN, preferred_element_type=F32)
    for i in range(3):
        out_ref[pl.ds(i, rows, stride=3), :] = result[:, i * head : (i + 1) * head]


def head_sum_kernel(dims, *rest):
    n_seq, blk = dims
    pair_refs, (out_ref, all_ref) = rest[:n_seq], rest[n_seq:]
    me = lax.axis_index("seq")
    for m in range(n_seq):
        pair_ref = pair_refs[m // 2 + (m % 2) * (n_seq // 2)]
        all_ref[me ^ m] = pair_ref[m % 2, blk:].astype(F32)
    total = all_ref[0]
    for h in range(1, n_seq):
        total = total + all_ref[h]
    out_ref[...] = total[:8] + pltpu.roll(total, EXTRA - 2, 0)[:8]


def group_sum_kernel(dims, *rest):
    (n_dp,) = dims
    sum_refs, (out_ref, all_ref) = rest[:n_dp], rest[n_dp:]
    slab = lax.axis_index("dp")
    for m in range(n_dp):
        all_ref[slab ^ m] = sum_refs[m][...]
    total = all_ref[0]
    for g in range(1, n_dp):
        total = total + all_ref[g]
    out_ref[...] = total[:2]


def finish_kernel(dims, *rest):
    n_seq, blk, head = dims
    pair_refs, (out_ref,) = rest[:n_seq], rest[n_seq:]
    me = lax.axis_index("seq")
    for m in range(n_seq):
        at = pl.multiple_of((me ^ m) * head, head)
        pair_ref = pair_refs[m // 2 + (m % 2) * (n_seq // 2)]
        out_ref[:, pl.ds(at, head)] = pair_ref[m % 2, :blk]


def body(
    features,
    conv_weight,
    clip_frames,
    clip_group,
    clip_offset,
    clip_times,
    noise_tokens,
    embed_weight,
    attention_proj,
    norm_gains,
    cotangent,
):
    n_dp, n_seq = lax.axis_size("dp"), lax.axis_size("seq")
    fr, rows_dev, wd, ch = features.shape
    lat = conv_weight.shape[3]
    clips = clip_frames.shape[0]
    cols = wd // 2
    blk, patch = noise_tokens.shape[1:]
    model, _, heads_dev, head = attention_proj.shape
    assert rows_dev == 2 and heads_dev == 1 and blk == fr * cols and patch == 4 * lat
    size = n_seq * blk
    lanes = len(CELLS) * lat
    S = jax.ShapeDtypeStruct

    rows_out = (fr + 2) * cols
    tile = min(512, size)

    partial = pl.pallas_call(
        functools.partial(conv_kernel, (fr, wd, ch, lat, clips)),
        out_shape=S((rows_out, lanes), BF16),
        in_specs=[HBM] * 3,
        out_specs=VMEM,
        scratch_shapes=[
            pltpu.SMEM((clips,), jnp.int32),
            pltpu.VMEM((fr * 2 * wd, ch), BF16),
            pltpu.VMEM((27 * lat, ch), BF16),
            pltpu.VMEM((ch // 128, fr * 2 * wd, 128), F32),
            pltpu.VMEM((4, 6 * lanes, ch), BF16),
            pltpu.SemaphoreType.DMA((3,)),
        ],
        compiler_params=params(),
        cost_estimate=cost(2 * fr * cols * 4 * ch * 6 * lanes, 2**21, fr * 2 * wd * ch),
        name="conv",
    )(
        *keep_in(
            pltpu.HBM,
            clip_frames,
            features.reshape(fr * 2 * wd, ch),
            conv_weight.reshape(27 * lat, ch),
        )
    )
    parts = [partial] + [swap(partial, "dp", m) for m in range(1, n_dp)]
    half = n_seq // 2
    cots = pl.pallas_call(
        functools.partial(split_kernel, (n_seq, head)),
        out_shape=[S((2, blk, head), BF16)] * half,
        in_specs=[VMEM] * 2,
        out_specs=[VMEM] * half,
        compiler_params=params(),
        cost_estimate=cost(0, 4 * blk * n_seq * head),
        name="split",
    )(partial, cotangent.reshape(blk, n_seq * head))
    cots = [cots[0]] + [swap(cots[m], "seq", 2 * m) for m in range(1, half)]
    cots += [swap(pair, "seq", 1) for pair in cots]
    pick, scale, noise, live, mark = pl.pallas_call(
        functools.partial(table_kernel, (fr, cols, clips, n_dp, patch, lanes)),
        out_shape=[S((blk, n_dp * rows_out), BF16)] + [S((blk, lanes), F32)] * 4,
        in_specs=[SMEM] * 4 + [VMEM] * 2,
        out_specs=[VMEM] * 5,
        compiler_params=params(),
        cost_estimate=cost(2**22, 2**21),
        name="tables",
    )(clip_frames, clip_group, clip_offset, clip_times, partial, noise_tokens[0].T)

    send, own = pl.pallas_call(
        functools.partial(slot_kernel, (n_dp,)),
        out_shape=[S((blk, lanes), BF16), S((blk, lanes), F32)],
        in_specs=[VMEM] * (3 + n_dp),
        out_specs=[VMEM] * 2,
        compiler_params=params(),
        cost_estimate=cost(2**20, 2**18),
        name="slots",
    )(pick, scale, noise, *parts)
    toks = [send] + [None] * (n_seq - 1)
    for m in range(2, n_seq, 2):
        toks[m] = swap(send, "seq", m)
    for m in range(0, n_seq, 2):
        toks[m + 1] = swap(toks[m], "seq", 1)
    weights = pl.pallas_call(
        functools.partial(weight_kernel, (patch, head)),
        out_shape=S((4 * patch, 3 * head), BF16),
        in_specs=[VMEM] * 3,
        out_specs=VMEM,
        compiler_params=params(),
        cost_estimate=cost(2 * patch * model * 3 * head, 2 * model * (3 * head + patch)),
        name="weights",
    )(send, embed_weight, attention_proj.transpose(1, 2, 0, 3).reshape(3, model, head))

    wide = 2 * head
    noisy, grad, *pairs = pl.pallas_call(
        functools.partial(attention_kernel, (fr, cols, n_seq, patch, head, tile)),
        out_shape=[S((patch, blk), F32), S((patch, 3 * head), BF16)]
        + [S((2, blk + EXTRA, head), BF16)] * half,
        in_specs=[VMEM] * (5 + 2 * n_seq),
        out_specs=[VMEM] * (2 + half),
        scratch_shapes=[
            pltpu.VMEM((size + 2 * blk, lanes), BF16),
            pltpu.VMEM((size, head), BF16),
            pltpu.VMEM((size, 2 * lanes), BF16),
            pltpu.VMEM((size, wide), F32),
            pltpu.VMEM((size, wide), F32),
            pltpu.VMEM((size, wide), BF16),
            pltpu.VMEM((size, wide), BF16),
            pltpu.VMEM((size, wide), BF16),
            pltpu.VMEM((size, head), BF16),
            pltpu.VMEM((size, head), F32),
            pltpu.VMEM((size, head), F32),
            pltpu.VMEM((size, head), F32),
        ],
        compiler_params=params(),
        cost_estimate=cost(12 * size * size * head, 2**21, size * size),
        name="attention",
    )(norm_gains, weights, own, live, mark, *toks, *cots)

    pairs = [pairs[0]] + [swap(pairs[m], "seq", 2 * m) for m in range(1, half)]
    grads = [grad] + [swap(grad, "dp", m) for m in range(1, n_dp)]
    pairs += [swap(pair, "seq", 1) for pair in pairs]
    gain = pl.pallas_call(
        functools.partial(head_sum_kernel, (n_seq, blk)),
        out_shape=S((8, head), F32),
        in_specs=[VMEM] * n_seq,
        out_specs=VMEM,
        scratch_shapes=[pltpu.VMEM((n_seq, EXTRA, head), F32)],
        compiler_params=params(),
        cost_estimate=cost(0, 2**12),
        name="headsum",
    )(*pairs)
    gain = [gain] + [swap(gain, "dp", m) for m in range(1, n_dp)]
    norm_grad = pl.pallas_call(
        functools.partial(group_sum_kernel, (n_dp,)),
        out_shape=S((2, head), F32),
        in_specs=[VMEM] * n_dp,
        out_specs=VMEM,
        scratch_shapes=[pltpu.VMEM((n_dp, 8, head), F32)],
        compiler_params=params(),
        cost_estimate=cost(0, 2**12),
        name="groupsum",
    )(*gain)
    rows = model // n_dp
    proj_grad = pl.pallas_call(
        functools.partial(proj_kernel, (n_dp, patch, head, rows)),
        out_shape=S((rows * 3, head), F32),
        in_specs=[VMEM] * (1 + n_dp),
        out_specs=VMEM,
        compiler_params=params(),
        cost_estimate=cost(2 * rows * 3 * head * patch * n_dp, 4 * rows * 3 * head),
        name="projgrad",
    )(embed_weight, *grads)
    out = pl.pallas_call(
        functools.partial(finish_kernel, (n_seq, blk, head)),
        out_shape=S((blk, n_seq * head), BF16),
        in_specs=[VMEM] * n_seq,
        out_specs=VMEM,
        compiler_params=params(),
        cost_estimate=cost(0, 4 * blk * n_seq * head),
        name="finish",
    )(*pairs)
    return (
        noisy.T[None],
        out[None],
        proj_grad.reshape(rows, 3, heads_dev, head),
        norm_grad,
    )


def solution(mesh):
    return jax.shard_map(
        body,
        mesh=mesh,
        in_specs=(
            P("dp", "seq", None, None),
            P(),
            P(),
            P(),
            P(),
            P(),
            P("dp", "seq", None),
            P(),
            P(None, None, "seq", None),
            P(),
            P("dp", "seq", None),
        ),
        out_specs=(P("dp", "seq", None), P("dp", "seq", None), P("dp", None, "seq", None), P()),
        check_vma=False,
    )
```
